256 devices in a mesh: sub: 2 (over x_lo), row: 8 (over y, x_hi), col: 16 (over z, core).
Axes of the slice: x: 4 (x_hi: 2, x_lo: 2; x = x_hi * 2 + x_lo), y: 4, z: 8, core: 2. Of those that a mesh axis runs over, the one named last changes fastest.
Arguments:
- front: float32 [10240, 10240], P(('sub', 'row'), 'col')
- children: float32 [4, 6144, 6144], P('sub', 'row', 'col')
- child_maps: int32 [4, 48], replicated, may hold values from 0 to 79, as said below
Outputs:
- factored: float32 [10240, 10240], P(('sub', 'row'), 'col')
The draws below stay inside these ranges and needn't reach their ends.
Inputs may be any that keep to these rules, and one draw needn't show every extreme that they name: `child_maps`: each row holds 48 different parent block numbers, and entry i leaves the same remainder as i on division by 16. Child 0 sends its block 0 to parent block 0, child 1 its last block to parent block 79.
All inputs are finite; a program needn't handle non-finite values.
Results may differ from the reference program's by a relative error of at most 0.0001.
Values sent between devices are 32-bit elements; how exact they have to be, the bound alone decides.
A program may use at most 64 MiB of HBM per device.

```python
import math
import jax
import jax.numpy as jnp
from jax import lax

BS = 128
NF = 10240
NC = 6144
P_SIZE = 384
CHILDREN = 4
ROWDEV = 16
CHILD_ROWDEV = 8
COLDEV = 16
NFB = 80
NCB = 48
NPB = 3


def to_stored_drawn(logical, rdev, cdev):
    row_count, col_count = logical.shape
    result = logical.reshape(row_count // (rdev * BS), rdev, BS, col_count).transpose(1, 0, 2, 3).reshape(row_count, col_count)
    result = result.reshape(row_count, col_count // (cdev * BS), cdev, BS).transpose(0, 2, 1, 3).reshape(row_count, col_count)
    return result


def make_maps(key):
    map_key = jax.random.fold_in(key, 7)
    slot_count = NFB // COLDEV
    pick_count = NCB // COLDEV
    random_keys = jax.random.randint(map_key, (CHILDREN, COLDEV, slot_count), 0, 1 << 20)
    scores = random_keys * slot_count + jnp.arange(slot_count, dtype=jnp.int32)
    scores = scores.at[0, 0, 0].set(-1)
    scores = scores.at[1, COLDEV - 1, slot_count - 1].set(-1)
    ranked = jnp.argsort(scores, axis=-1, stable=True)
    chosen = jnp.sort(ranked[:, :, :pick_count], axis=-1).astype(jnp.int32)
    blocks = jnp.arange(COLDEV, dtype=jnp.int32)[None, :, None] + COLDEV * chosen
    return jnp.transpose(blocks, (0, 2, 1)).reshape(CHILDREN, NCB).astype(jnp.int32)


def symmetric(values):
    return jnp.tril(values) + jnp.tril(values, -1).T


def regional(key, is_pivot, tiny, middle):
    key_unit, key_wide = jax.random.split(key)
    count = is_pivot.shape[0]
    bounded = jax.random.uniform(key_unit, (count, count), jnp.float32, -1.0, 1.0)
    normal_vals = jnp.clip(jax.random.normal(key_wide, (count, count), jnp.float32), -4.0, 4.0)
    both_pivot = is_pivot[:, None] & is_pivot[None, :]
    one_pivot = is_pivot[:, None] != is_pivot[None, :]
    values = jnp.where(both_pivot, bounded * tiny, jnp.where(one_pivot, normal_vals * middle, normal_vals))
    return symmetric(values)


def pivot_coupling(key):
    integer_factors = jax.random.randint(key, (P_SIZE, P_SIZE), -2, 3).astype(jnp.int32)
    gram_matrix = jnp.dot(integer_factors, integer_factors.T, preferred_element_type=jnp.int32)
    strength = 0.5 / P_SIZE
    return gram_matrix.astype(jnp.float32) * strength


def draw_front(key, part):
    indices = jnp.arange(NF, dtype=jnp.int32)
    is_pivot = indices < P_SIZE
    values = regional(jax.random.fold_in(key, 1), is_pivot, 0.9 / P_SIZE, 3.0 / math.sqrt(P_SIZE))
    key_pivot, key_trail = jax.random.split(jax.random.fold_in(key, 2))
    diag_vals = jnp.where(is_pivot, jax.random.uniform(key_pivot, (NF,), jnp.float32, 1.5, 2.0), jax.random.uniform(key_trail, (NF,), jnp.float32, 6.0, 10.0))
    logical = jnp.where(indices[:, None] == indices[None, :], diag_vals[:, None], values)
    logical = logical.at[:P_SIZE, :P_SIZE].add(pivot_coupling(jax.random.fold_in(key, 3)))
    return to_stored_drawn(logical, ROWDEV, COLDEV)


def draw_children(key, part):
    maps = make_maps(key)
    stacked = []
    for child in range(CHILDREN):
        owner_blocks = maps[child][jnp.arange(NC, dtype=jnp.int32) // BS]
        is_pivot = owner_blocks < NPB
        values = regional(jax.random.fold_in(key, 100 + child), is_pivot, 0.1 / P_SIZE, 1.5 / math.sqrt(P_SIZE))
        stacked.append(to_stored_drawn(values, CHILD_ROWDEV, COLDEV))
    return jnp.stack(stacked)


def draw_child_maps(key, part):
    return make_maps(key)


def setup_inputs(seed: int = 0) -> dict:
    arg_keys = jax.random.split(jax.random.key(seed), 4)
    front = draw_front(jax.random.fold_in(arg_keys[3], 71), 0)
    children = draw_children(jax.random.fold_in(arg_keys[3], 71), 0)
    child_maps = draw_child_maps(jax.random.fold_in(arg_keys[3], 71), 0)
    return dict(front=front, children=children, child_maps=child_maps)


def to_logical(stored, rdev, cdev):
    row_count, col_count = stored.shape
    result = stored.reshape(rdev, row_count // (rdev * BS), BS, col_count).transpose(1, 0, 2, 3).reshape(row_count, col_count)
    result = result.reshape(row_count, cdev, col_count // (cdev * BS), BS).transpose(0, 2, 1, 3).reshape(row_count, col_count)
    return result

def to_stored(logical, rdev, cdev):
    row_count, col_count = logical.shape
    result = logical.reshape(row_count // (rdev * BS), rdev, BS, col_count).transpose(1, 0, 2, 3).reshape(row_count, col_count)
    result = result.reshape(row_count, col_count // (cdev * BS), cdev, BS).transpose(0, 2, 1, 3).reshape(row_count, col_count)
    return result

def reference(front, children, child_maps):
    matrix = to_logical(front, ROWDEV, COLDEV)
    tiles = matrix.reshape(NFB, BS, NFB, BS).transpose(0, 2, 1, 3)
    for child in range(CHILDREN):
        update = to_logical(children[child], CHILD_ROWDEV, COLDEV)
        update = update.reshape(NCB, BS, NCB, BS).transpose(0, 2, 1, 3)
        targets = child_maps[child].astype(jnp.int32)
        tiles = tiles.at[targets[:, None], targets[None, :]].add(update)
    matrix = tiles.transpose(0, 2, 1, 3).reshape(NF, NF)
    blocks = jnp.arange(NF, dtype=jnp.int32) // BS
    identity = jnp.eye(BS, dtype=jnp.float32)
    highest = lax.Precision.HIGHEST

    def eliminate(section, matrix):
        section = section.astype(jnp.int32)
        position = section * BS
        corner = lax.dynamic_slice(matrix, (position, position), (BS, BS))
        factor = jnp.linalg.cholesky(corner)
        inverse = jax.scipy.linalg.solve_triangular(factor, identity, lower=True)
        column = lax.dynamic_slice_in_dim(matrix, position, BS, 1)
        panel_rows = jnp.dot(column, inverse.T, precision=highest)
        below_mask = (blocks > section)[:, None]
        left_factor = jnp.where(below_mask, panel_rows, 0.0)
        matrix = matrix - jnp.dot(left_factor, left_factor.T, precision=highest)
        lower_tile = jnp.tile(jnp.tril(factor), (NFB, 1))
        written = jnp.where(below_mask, panel_rows, jnp.where((blocks == section)[:, None], lower_tile, 0.0))
        matrix = lax.dynamic_update_slice_in_dim(matrix, written, position, 1)
        row_strip = lax.dynamic_slice_in_dim(matrix, position, BS, 0)
        row_strip = jnp.where((blocks > section)[None, :], 0.0, row_strip)
        return lax.dynamic_update_slice_in_dim(matrix, row_strip, position, 0)
    matrix = lax.fori_loop(0, NPB, eliminate, matrix)
    return to_stored(matrix, ROWDEV, COLDEV)
```

```python
import jax
import jax.numpy as jnp
from jax import lax
from jax.experimental import pallas as pl
from jax.experimental.pallas import tpu as pltpu
from jax.sharding import PartitionSpec as P

BS = 128
NPB = 3
LEAF = 8
F32 = jnp.float32
MESH = pl.DeviceIdType.MESH
HIGHEST = lax.Precision.HIGHEST
VMEM = pl.BlockSpec(memory_space=pltpu.VMEM)
SMEM = pl.BlockSpec(memory_space=pltpu.SMEM)
SOURCE = ((0, 0, 1), (2, 0, -1), (0, 1, 1))


def position():
    return lax.axis_index("sub"), lax.axis_index("row"), lax.axis_index("col")


def dot(a, b, dims):
    return lax.dot_general(a, b, (dims, ((), ())), precision=HIGHEST, preferred_element_type=F32)


def row_target(maps, child, local, row):
    return maps[child, local * 8 + row] // 16


def col_target(maps, child, m, col):
    return maps[child, m * 16 + col] // 16


def tile(ref, a, b):
    return ref.at[pl.ds(pl.multiple_of(a * BS, BS), BS), pl.ds(pl.multiple_of(b * BS, BS), BS)]


def prepare_kernel(maps, front, children, col_send, col_mine, row_send, row_mine, bulk):
    s, r, q = position()

    def block(c, local, m):
        return children[c, pl.ds(pl.multiple_of(local * BS, BS), BS), m * BS : (m + 1) * BS]

    @pl.when(q < NPB)
    def _():
        for n in range(5):
            col_mine[n] = front[n * BS : (n + 1) * BS, :BS]
            col_send[n] = jnp.zeros((BS, BS), F32)
        for c in range(2):
            for m in range(3):

                @pl.when(col_target(maps, 2 * s + c, m, q) == 0)
                def _():
                    for u in range(3):
                        a = row_target(maps, 2 * s + c, 2 * u + s, r)
                        col_mine[a] = col_mine[a] + block(c, 2 * u + s, m)
                        a = row_target(maps, 2 * s + c, 2 * u + 1 - s, r)
                        col_send[a] = col_send[a] + block(c, 2 * u + 1 - s, m)

    @pl.when(r < NPB)
    def _():
        for n in range(5):
            row_mine[n] = front[:BS, n * BS : (n + 1) * BS]
            row_send[n] = jnp.zeros((BS, BS), F32)
        for c in range(2):
            for u in range(3):

                @pl.when(row_target(maps, 2 * s + c, 2 * u, r) == 0)
                def _():
                    for m in range(3):
                        b = col_target(maps, 2 * s + c, m, q)

                        @pl.when(s == 0)
                        def _():
                            row_mine[b] = row_mine[b] + block(c, 2 * u, m)

                        @pl.when(s == 1)
                        def _():
                            row_send[b] = row_send[b] + block(c, 2 * u, m)

    for c in range(2):
        for u in range(3):
            bulk[c, u] = children[c, pl.ds(pl.multiple_of((2 * u + 1 - s) * BS, BS), BS), :]


def spread_kernel(col_send, col_mine, row_send, row_mine, left, right, corner,
                  col_recv, row_recv, xs, xr, zs, zr, ys, yr):
    s, r, q = position()
    x, y, z, core = 2 * lax.rem(r, 2) + s, r // 2, q // 2, lax.rem(q, 2)

    def at_x(d):
        nx = lax.rem(x + 4 + d, 4)
        return (lax.rem(nx, 2), 2 * y + nx // 2, q)

    def at_y(d):
        return (s, 2 * lax.rem(y + 4 + d, 4) + lax.rem(r, 2), q)

    def at_z(d):
        return (s, r, 2 * lax.rem(z + 8 + d, 8) + core)

    sibling = (s, r, 2 * z + 1 - core)
    partner = (1 - s, r, q)

    barrier = pltpu.get_barrier_semaphore()
    for peer in (at_x(1), at_x(-1), at_y(1), at_y(-1), at_z(1), at_z(-1), sibling):
        pl.semaphore_signal(barrier, inc=1, device_id=peer, device_id_type=MESH)
    pl.semaphore_wait(barrier, 7)

    def copy(src, dst, send, recv, device):
        return pltpu.make_async_remote_copy(
            src_ref=src, dst_ref=dst, send_sem=send, recv_sem=recv, device_id=device, device_id_type=MESH
        )

    def col_copy(n):
        return copy(col_send.at[n], col_recv.at[n], xs.at[0, n], xr.at[0, n], partner)

    def row_copy(n):
        return copy(row_send.at[n], row_recv.at[n], xs.at[1, n], xr.at[1, n], partner)

    col_on = q < NPB
    row_out = (r < NPB) & (s == 1)

    def exchange(act):
        @pl.loop(0, 5)
        def _(n):
            @pl.when(col_on)
            def _():
                act(col_copy(n))

            @pl.when(row_out)
            def _():
                act(row_copy(n))

    exchange(lambda c: c.start())

    def line_sends(k, n, act):
        zk, ck = k // 2, k % 2
        dz = lax.rem(z - zk + 8, 8)
        on = core == ck
        here = left.at[k, n]

        @pl.when(on & (dz <= 3))
        def _():
            act(copy(here, here, zs.at[k, n, 0], zr.at[k, n], at_z(1)))

        @pl.when(on & ((dz == 0) | (dz >= 6)))
        def _():
            act(copy(here, here, zs.at[k, n, 1], zr.at[k, n], at_z(-1)))

        @pl.when(on)
        def _():
            act(copy(here, here, zs.at[k, n, 2], zr.at[k, n], sibling))

    def line_step(k, n):
        @pl.when(q == k)
        def _():
            col_copy(n).wait_recv()
            left[k, n] = col_mine[n] + col_recv[n]

        @pl.when(q != k)
        def _():
            copy(left.at[k, n], left.at[k, n], zs.at[k, n, 0], zr.at[k, n], sibling).wait_recv()

        line_sends(k, n, lambda c: c.start())

    def offsets(i):
        xi, yi, g = SOURCE[i]
        return lax.rem(g * (x - xi) + 4, 4), lax.rem(y - yi + 4, 4), g

    def plane_sends(i, here, slot, act):
        dx, dy, g = offsets(i)
        along_x = (core == 1) | (dy == 0)
        along_y = (core == 0) | (dx == 0)

        @pl.when(along_x & (dx <= 1))
        def _():
            act(copy(here, here, ys.at[i, slot, 0], yr.at[i, slot], at_x(g)))

        @pl.when(along_x & (dx == 0))
        def _():
            act(copy(here, here, ys.at[i, slot, 1], yr.at[i, slot], at_x(-g)))

        @pl.when(along_y & (dy <= 1))
        def _():
            act(copy(here, here, ys.at[i, slot, 2], yr.at[i, slot], at_y(1)))

        @pl.when(along_y & (dy == 0))
        def _():
            act(copy(here, here, ys.at[i, slot, 3], yr.at[i, slot], at_y(-1)))

    def plane_step(i, here, slot, make):
        dx, dy, _ = offsets(i)
        source = (dx == 0) & (dy == 0)
        pl.when(source)(make)

        @pl.when(jnp.logical_not(source))
        def _():
            copy(here, here, ys.at[i, slot, 0], yr.at[i, slot], sibling).wait_recv()

        plane_sends(i, here, slot, lambda c: c.start())

    def row_make(i, n):
        def make():
            row_copy(n).wait_recv()
            right[i, n] = row_mine[n] + row_recv[n]

        return make

    def corner_make(i, k):
        def make():
            corner[i, k] = left[k, 0]

        return make

    corners = [(i, k) for i in range(NPB) for k in range(i + 1)]
    for k in range(NPB):
        line_step(k, 0)
    for i, k in corners:
        plane_step(i, corner.at[i, k], 5 + k, corner_make(i, k))
    for i in range(NPB):
        plane_step(i, right.at[i, 0], 0, row_make(i, 0))

    @pl.loop(1, 5)
    def _(n):
        for k in range(NPB):
            line_step(k, n)
        for i in range(NPB):
            plane_step(i, right.at[i, n], n, row_make(i, n))

    exchange(lambda c: c.wait_send())
    for i, k in corners:
        plane_sends(i, corner.at[i, k], 5 + k, lambda c: c.wait_send())

    @pl.loop(0, 5)
    def _(n):
        for k in range(NPB):
            line_sends(k, n, lambda c: c.wait_send())
        for i in range(NPB):
            plane_sends(i, right.at[i, n], n, lambda c: c.wait_send())


def lanes(v, j):
    return jnp.take_along_axis(v, jnp.full((8, BS), j, jnp.int32), axis=1)


def sublanes(v, i):
    return jnp.broadcast_to(v[i : i + 1, :], (8, BS))


def factor_block(block):
    row = lax.broadcasted_iota(jnp.int32, (8, BS), 0)
    lane = lax.broadcasted_iota(jnp.int32, (8, BS), 1)
    tiles = BS // LEAF
    wa = [block[8 * t : 8 * t + 8] for t in range(tiles)]
    wi = [jnp.where(lane == row + 8 * t, 1.0, 0.0).astype(F32) for t in range(tiles)]
    upper, inverse = [], []
    for t in range(tiles):
        cols = {w: [lanes(wa[w], 8 * t + m) for m in range(8)] for w in range(t, tiles)}
        sc = [[sublanes(cols[t][n], m) if n <= m else None for n in range(8)] for m in range(8)]
        low = [[None] * 8 for _ in range(8)]
        rs, ua, ui = [None] * 8, [None] * 8, [None] * 8
        for m in range(8):
            rs[m] = lax.rsqrt(sc[m][m])
            for i in range(m + 1, 8):
                low[i][m] = sc[i][m] * rs[m]
            for i in range(m + 1, 8):
                for j in range(m + 1, i + 1):
                    sc[i][j] = sc[i][j] - low[i][m] * low[j][m]
            ga, gi = sublanes(wa[t], m), sublanes(wi[t], m)
            for n in range(m):
                ga = ga - low[m][n] * ua[n]
                gi = gi - low[m][n] * ui[n]
            ua[m], ui[m] = ga * rs[m], gi * rs[m]
        up, inv = ua[0], ui[0]
        for m in range(1, 8):
            up = jnp.where(row == m, ua[m], up)
            inv = jnp.where(row == m, ui[m], inv)
        upper.append(jnp.where(lane >= row + 8 * t, up, 0.0))
        inverse.append(jnp.where(lane <= row + 8 * t, inv, 0.0))
        if t == tiles - 1:
            break
        ya, yi = [None] * 8, [None] * 8
        for m in reversed(range(8)):
            a, b = ua[m], ui[m]
            for n in range(m + 1, 8):
                a = a - low[n][m] * ya[n]
                b = b - low[n][m] * yi[n]
            ya[m], yi[m] = a * rs[m], b * rs[m]
        for w in range(t + 1, tiles):
            a, b = wa[w], wi[w]
            for m in range(8):
                a = a - cols[w][m] * ya[m]
                b = b - cols[w][m] * yi[m]
            wa[w], wi[w] = a, b
    return jnp.concatenate(upper, 0), jnp.concatenate(inverse, 0)


ROWS_T = ((1,), (1,))
PLAIN = ((1,), (0,))


def place(maps, base, c, s, r, q, local, read):
    for u in range(3):
        a = row_target(maps, c, local(u), r)
        for m in range(3):
            b = col_target(maps, c, m, q)
            t = tile(base, a, b)
            t[...] = t[...] + read(u, m)


def factor_kernel(maps, corner, left, right, front, children, panel, upper, base, pr):
    s, r, q = position()
    d = {(i, k): corner[i, k] for i in range(NPB) for k in range(i + 1)}
    for k in range(NPB):
        up, inv = factor_block(d[k, k])
        upper[k] = up
        low = {}
        for i in range(k + 1, NPB):
            low[i] = dot(d[i, k], inv, ROWS_T)
        for i in range(k + 1, NPB):
            for j in range(k + 1, i + 1):
                d[i, j] = d[i, j] - dot(low[i], low[j], ROWS_T)
        mine = left[k].reshape(5 * BS, BS)
        for i in range(k):
            mine = mine - dot(panel[:, i * BS : (i + 1) * BS], lows[k, i], ROWS_T)
        panel[:, k * BS : (k + 1) * BS] = dot(mine, inv, ROWS_T)
        for n in range(5):
            other = right[k, n]
            for i in range(k):
                other = other - dot(lows[k, i], pr[i * BS : (i + 1) * BS, n * BS : (n + 1) * BS], PLAIN)
            pr[k * BS : (k + 1) * BS, n * BS : (n + 1) * BS] = dot(inv, other, PLAIN)
        if k == 0:
            lows = {}
        for i in low:
            lows[i, k] = low[i]

    for a in range(5):
        rows = slice(a * BS, (a + 1) * BS)
        base[rows, :] = front[rows, :] - dot(panel[rows, :], pr[...], PLAIN)
    for c in range(2):
        place(
            maps, base, 2 * s + c, s, r, q, lambda u: 2 * u + s,
            lambda u, m: children[c, pl.ds(pl.multiple_of((2 * u + s) * BS, BS), BS), m * BS : (m + 1) * BS],
        )


def finish_kernel(maps, base, arrived, panel, upper, out):
    s, r, q = position()
    dev_row = 8 * s + r
    out[...] = base[...]
    for c in range(2):
        place(
            maps, out, 2 * (1 - s) + c, s, r, q, lambda u: 2 * u + s,
            lambda u, m: arrived[c, u, :, m * BS : (m + 1) * BS],
        )

    @pl.when(q < NPB)
    def _():
        lane = pl.ds(pl.multiple_of(q * BS, BS), BS)
        out[BS:, :BS] = panel[BS:, lane]

        @pl.when(dev_row > q)
        def _():
            out[:BS, :BS] = panel[:BS, lane]

        @pl.when(dev_row == q)
        def _():
            out[:BS, :BS] = upper[q].T

    @pl.when(dev_row < NPB)
    def _():
        out[:BS, BS:] = jnp.zeros((BS, 4 * BS), F32)

        @pl.when(q > dev_row)
        def _():
            out[:BS, :BS] = jnp.zeros((BS, BS), F32)


def shape(*dims):
    return jax.ShapeDtypeStruct(dims, F32)


def body(front, children, child_maps):
    col_send, col_mine, row_send, row_mine, bulk = pl.pallas_call(
        prepare_kernel,
        out_shape=[shape(5, BS, BS)] * 4 + [shape(2, 3, BS, 3 * BS)],
        in_specs=[SMEM, VMEM, VMEM],
        out_specs=[VMEM] * 5,
        name="prepare",
    )(child_maps, front, children)
    dma = pltpu.SemaphoreType.DMA
    left, right, corner = pl.pallas_call(
        spread_kernel,
        out_shape=[shape(NPB, 5, BS, BS), shape(NPB, 5, BS, BS), shape(NPB, NPB, BS, BS)],
        in_specs=[VMEM] * 4,
        out_specs=[VMEM] * 3,
        scratch_shapes=[
            pltpu.VMEM((5, BS, BS), F32),
            pltpu.VMEM((5, BS, BS), F32),
            dma((2, 5)),
            dma((2, 5)),
            dma((NPB, 5, 3)),
            dma((NPB, 5)),
            dma((NPB, 8, 4)),
            dma((NPB, 8)),
        ],
        compiler_params=pltpu.CompilerParams(collective_id=0, has_side_effects=True),
        name="spread",
    )(col_send, col_mine, row_send, row_mine)
    bulk, corner = lax.optimization_barrier((bulk, corner))
    arrived = lax.ppermute(bulk, "sub", [(0, 1), (1, 0)])
    panel, upper, base = pl.pallas_call(
        factor_kernel,
        out_shape=[shape(5 * BS, NPB * BS), shape(NPB, BS, BS), shape(5 * BS, 5 * BS)],
        in_specs=[SMEM] + [VMEM] * 5,
        out_specs=[VMEM] * 3,
        scratch_shapes=[pltpu.VMEM((NPB * BS, 5 * BS), F32)],
        cost_estimate=pl.CostEstimate(flops=10**10, bytes_accessed=10**8, transcendentals=0),
        name="factor",
    )(child_maps, corner, left, right, front, children)
    return pl.pallas_call(
        finish_kernel,
        out_shape=shape(5 * BS, 5 * BS),
        in_specs=[SMEM] + [VMEM] * 4,
        out_specs=VMEM,
        name="finish",
    )(child_maps, base, arrived, panel, upper)


def solution(mesh):
    return jax.shard_map(
        body,
        mesh=mesh,
        in_specs=(P(("sub", "row"), "col"), P("sub", "row", "col"), P()),
        out_specs=P(("sub", "row"), "col"),
        check_vma=False,
    )
```

```python
import jax
import jax.numpy as jnp
from jax import lax
from jax.experimental import pallas as pl
from jax.experimental.pallas import tpu as pltpu
from jax.sharding import PartitionSpec as P

BS = 128
NPB = 3
LEAF = 8
F32 = jnp.float32
MESH = pl.DeviceIdType.MESH
HIGHEST = lax.Precision.HIGHEST
VMEM = pl.BlockSpec(memory_space=pltpu.VMEM)
SMEM = pl.BlockSpec(memory_space=pltpu.SMEM)
SOURCE = ((0, 0, 1), (2, 0, -1), (0, 1, 1))


def position():
    return lax.axis_index("sub"), lax.axis_index("row"), lax.axis_index("col")


def dot(a, b, dims):
    return lax.dot_general(a, b, (dims, ((), ())), precision=HIGHEST, preferred_element_type=F32)


def row_target(maps, child, local, row):
    return maps[child, local * 8 + row] // 16


def col_target(maps, child, m, col):
    return maps[child, m * 16 + col] // 16


def tile(ref, a, b):
    return ref.at[pl.ds(pl.multiple_of(a * BS, BS), BS), pl.ds(pl.multiple_of(b * BS, BS), BS)]


def prepare_kernel(maps, front, children, col_send, col_mine, row_send, row_mine, bulk):
    s, r, q = position()

    def block(c, local, m):
        return children[c, pl.ds(pl.multiple_of(local * BS, BS), BS), m * BS : (m + 1) * BS]

    @pl.when(q < NPB)
    def _():
        for n in range(5):
            col_mine[n] = front[n * BS : (n + 1) * BS, :BS]
            col_send[n] = jnp.zeros((BS, BS), F32)
        for c in range(2):
            for m in range(3):

                @pl.when(col_target(maps, 2 * s + c, m, q) == 0)
                def _():
                    for u in range(3):
                        a = row_target(maps, 2 * s + c, 2 * u + s, r)
                        col_mine[a] = col_mine[a] + block(c, 2 * u + s, m)
                        a = row_target(maps, 2 * s + c, 2 * u + 1 - s, r)
                        col_send[a] = col_send[a] + block(c, 2 * u + 1 - s, m)

    @pl.when(r < NPB)
    def _():
        for n in range(5):
            row_mine[n] = front[:BS, n * BS : (n + 1) * BS]
            row_send[n] = jnp.zeros((BS, BS), F32)
        for c in range(2):
            for u in range(3):

                @pl.when(row_target(maps, 2 * s + c, 2 * u, r) == 0)
                def _():
                    for m in range(3):
                        b = col_target(maps, 2 * s + c, m, q)

                        @pl.when(s == 0)
                        def _():
                            row_mine[b] = row_mine[b] + block(c, 2 * u, m)

                        @pl.when(s == 1)
                        def _():
                            row_send[b] = row_send[b] + block(c, 2 * u, m)

    for c in range(2):
        for u in range(3):
            bulk[c, u] = children[c, pl.ds(pl.multiple_of((2 * u + 1 - s) * BS, BS), BS), :]


def spread_kernel(col_send, col_mine, row_send, row_mine, left, right, corner,
                  col_recv, row_recv, xs, xr, zs, zr, ys, yr):
    s, r, q = position()
    x, y, z, core = 2 * lax.rem(r, 2) + s, r // 2, q // 2, lax.rem(q, 2)

    def at_x(d):
        nx = lax.rem(x + 4 + d, 4)
        return (lax.rem(nx, 2), 2 * y + nx // 2, q)

    def at_y(d):
        return (s, 2 * lax.rem(y + 4 + d, 4) + lax.rem(r, 2), q)

    def at_z(d):
        return (s, r, 2 * lax.rem(z + 8 + d, 8) + core)

    sibling = (s, r, 2 * z + 1 - core)
    partner = (1 - s, r, q)

    barrier = pltpu.get_barrier_semaphore()
    for peer in (at_x(1), at_x(-1), at_y(1), at_y(-1), at_z(1), at_z(-1), sibling):
        pl.semaphore_signal(barrier, inc=1, device_id=peer, device_id_type=MESH)
    pl.semaphore_wait(barrier, 7)

    def copy(src, dst, send, recv, device):
        return pltpu.make_async_remote_copy(
            src_ref=src, dst_ref=dst, send_sem=send, recv_sem=recv, device_id=device, device_id_type=MESH
        )

    def col_copy(n):
        return copy(col_send.at[n], col_recv.at[n], xs.at[0, n], xr.at[0, n], partner)

    def row_copy(n):
        return copy(row_send.at[n], row_recv.at[n], xs.at[1, n], xr.at[1, n], partner)

    col_on = q < NPB
    row_out = (r < NPB) & (s == 1)

    def exchange(act):
        @pl.loop(0, 5)
        def _(n):
            @pl.when(col_on)
            def _():
                act(col_copy(n))

            @pl.when(row_out)
            def _():
                act(row_copy(n))

    exchange(lambda c: c.start())

    def line_place(k):
        zk, ck = k // 2, k % 2
        dz = lax.rem(z - zk + 8, 8)
        on = core == ck
        hops = jnp.where(dz <= 4, dz, 8 - dz) + jnp.where(on, 0, 1)
        return dz, on, hops

    def line_sends(k, n, act):
        dz, on, _ = line_place(k)
        here = left.at[k, n]

        @pl.when(on & (dz <= 3))
        def _():
            act(copy(here, here, zs.at[k, n, 0], zr.at[k, n], at_z(1)))

        @pl.when(on & ((dz == 0) | (dz >= 6)))
        def _():
            act(copy(here, here, zs.at[k, n, 1], zr.at[k, n], at_z(-1)))

        @pl.when(on)
        def _():
            act(copy(here, here, zs.at[k, n, 2], zr.at[k, n], sibling))

    def line_step(k, n):
        @pl.when(q == k)
        def _():
            col_copy(n).wait_recv()
            left[k, n] = col_mine[n] + col_recv[n]

        @pl.when(q != k)
        def _():
            copy(left.at[k, n], left.at[k, n], zs.at[k, n, 0], zr.at[k, n], sibling).wait_recv()

        line_sends(k, n, lambda c: c.start())

    def plane_place(i):
        xi, yi, g = SOURCE[i]
        dx, dy = lax.rem(g * (x - xi) + 4, 4), lax.rem(g * (y - yi) + 4, 4)
        hops = jnp.where(dx == 3, 1, dx) + jnp.where(dy == 3, 1, dy)
        return dx, dy, g, hops

    def plane_sends(i, here, slot, act):
        dx, dy, g, _ = plane_place(i)
        along_x = (core == 1) | (dy == 0)
        along_y = (core == 0) | (dx == 0)

        @pl.when(along_x & (dx <= 1))
        def _():
            act(copy(here, here, ys.at[i, slot, 0], yr.at[i, slot], at_x(g)))

        @pl.when(along_x & (dx == 0))
        def _():
            act(copy(here, here, ys.at[i, slot, 1], yr.at[i, slot], at_x(-g)))

        @pl.when(along_y & (dy <= 1))
        def _():
            act(copy(here, here, ys.at[i, slot, 2], yr.at[i, slot], at_y(g)))

        @pl.when(along_y & (dy == 0))
        def _():
            act(copy(here, here, ys.at[i, slot, 3], yr.at[i, slot], at_y(-g)))

    def plane_step(i, here, slot, make):
        _, _, _, hops = plane_place(i)
        pl.when(hops == 0)(make)

        @pl.when(hops > 0)
        def _():
            copy(here, here, ys.at[i, slot, 0], yr.at[i, slot], sibling).wait_recv()

        plane_sends(i, here, slot, lambda c: c.start())

    def row_make(i, n):
        def make():
            row_copy(n).wait_recv()
            right[i, n] = row_mine[n] + row_recv[n]

        return make

    def corner_make(i, k):
        def make():
            corner[i, k] = left[k, 0]

        return make

    corners = [(i, k) for i in range(NPB) for k in range(i + 1)]

    @pl.loop(0, 10)
    def _(slot):
        for k in range(NPB):
            n = slot - line_place(k)[2]

            @pl.when((n >= 0) & (n < 5))
            def _():
                line_step(k, n)

        for i, k in corners:

            @pl.when(slot == line_place(k)[2] + plane_place(i)[3])
            def _():
                plane_step(i, corner.at[i, k], 5 + k, corner_make(i, k))

        for i in range(NPB):
            n = slot - plane_place(i)[3]

            @pl.when((n >= 0) & (n < 5))
            def _():
                plane_step(i, right.at[i, n], n, row_make(i, n))

    exchange(lambda c: c.wait_send())
    for i, k in corners:
        plane_sends(i, corner.at[i, k], 5 + k, lambda c: c.wait_send())

    @pl.loop(0, 5)
    def _(n):
        for k in range(NPB):
            line_sends(k, n, lambda c: c.wait_send())
        for i in range(NPB):
            plane_sends(i, right.at[i, n], n, lambda c: c.wait_send())


def lanes(v, j):
    return jnp.take_along_axis(v, jnp.full((8, BS), j, jnp.int32), axis=1)


def sublanes(v, i):
    return jnp.broadcast_to(v[i : i + 1, :], (8, BS))


def factor_block(block):
    row = lax.broadcasted_iota(jnp.int32, (8, BS), 0)
    lane = lax.broadcasted_iota(jnp.int32, (8, BS), 1)
    tiles = BS // LEAF
    wa = [block[8 * t : 8 * t + 8] for t in range(tiles)]
    wi = [jnp.where(lane == row + 8 * t, 1.0, 0.0).astype(F32) for t in range(tiles)]
    upper, inverse = [], []
    for t in range(tiles):
        cols = {w: [lanes(wa[w], 8 * t + m) for m in range(8)] for w in range(t, tiles)}
        sc = [[sublanes(cols[t][n], m) if n <= m else None for n in range(8)] for m in range(8)]
        low = [[None] * 8 for _ in range(8)]
        rs, ua, ui = [None] * 8, [None] * 8, [None] * 8
        for m in range(8):
            rs[m] = lax.rsqrt(sc[m][m])
            for i in range(m + 1, 8):
                low[i][m] = sc[i][m] * rs[m]
            for i in range(m + 1, 8):
                for j in range(m + 1, i + 1):
                    sc[i][j] = sc[i][j] - low[i][m] * low[j][m]
            ga, gi = sublanes(wa[t], m), sublanes(wi[t], m)
            for n in range(m):
                ga = ga - low[m][n] * ua[n]
                gi = gi - low[m][n] * ui[n]
            ua[m], ui[m] = ga * rs[m], gi * rs[m]
        up, inv = ua[0], ui[0]
        for m in range(1, 8):
            up = jnp.where(row == m, ua[m], up)
            inv = jnp.where(row == m, ui[m], inv)
        upper.append(jnp.where(lane >= row + 8 * t, up, 0.0))
        inverse.append(jnp.where(lane <= row + 8 * t, inv, 0.0))
        if t == tiles - 1:
            break
        ya, yi = [None] * 8, [None] * 8
        for m in reversed(range(8)):
            a, b = ua[m], ui[m]
            for n in range(m + 1, 8):
                a = a - low[n][m] * ya[n]
                b = b - low[n][m] * yi[n]
            ya[m], yi[m] = a * rs[m], b * rs[m]
        for w in range(t + 1, tiles):
            a, b = wa[w], wi[w]
            for m in range(8):
                a = a - cols[w][m] * ya[m]
                b = b - cols[w][m] * yi[m]
            wa[w], wi[w] = a, b
    return jnp.concatenate(upper, 0), jnp.concatenate(inverse, 0)


ROWS_T = ((1,), (1,))
PLAIN = ((1,), (0,))


def place(maps, base, c, s, r, q, local, read):
    for u in range(3):
        a = row_target(maps, c, local(u), r)
        for m in range(3):
            b = col_target(maps, c, m, q)
            t = tile(base, a, b)
            t[...] = t[...] + read(u, m)


def factor_kernel(maps, corner, left, right, front, children, panel, upper, base, pr):
    s, r, q = position()
    d = {(i, k): corner[i, k] for i in range(NPB) for k in range(i + 1)}
    for k in range(NPB):
        up, inv = factor_block(d[k, k])
        upper[k] = up
        low = {}
        for i in range(k + 1, NPB):
            low[i] = dot(d[i, k], inv, ROWS_T)
        for i in range(k + 1, NPB):
            for j in range(k + 1, i + 1):
                d[i, j] = d[i, j] - dot(low[i], low[j], ROWS_T)
        mine = left[k].reshape(5 * BS, BS)
        for i in range(k):
            mine = mine - dot(panel[:, i * BS : (i + 1) * BS], lows[k, i], ROWS_T)
        panel[:, k * BS : (k + 1) * BS] = dot(mine, inv, ROWS_T)
        for n in range(5):
            other = right[k, n]
            for i in range(k):
                other = other - dot(lows[k, i], pr[i * BS : (i + 1) * BS, n * BS : (n + 1) * BS], PLAIN)
            pr[k * BS : (k + 1) * BS, n * BS : (n + 1) * BS] = dot(inv, other, PLAIN)
        if k == 0:
            lows = {}
        for i in low:
            lows[i, k] = low[i]

    for a in range(5):
        rows = slice(a * BS, (a + 1) * BS)
        base[rows, :] = front[rows, :] - dot(panel[rows, :], pr[...], PLAIN)
    for c in range(2):
        place(
            maps, base, 2 * s + c, s, r, q, lambda u: 2 * u + s,
            lambda u, m: children[c, pl.ds(pl.multiple_of((2 * u + s) * BS, BS), BS), m * BS : (m + 1) * BS],
        )


def finish_kernel(maps, base, arrived, panel, upper, out):
    s, r, q = position()
    dev_row = 8 * s + r
    out[...] = base[...]
    for c in range(2):
        place(
            maps, out, 2 * (1 - s) + c, s, r, q, lambda u: 2 * u + s,
            lambda u, m: arrived[c, u, :, m * BS : (m + 1) * BS],
        )

    @pl.when(q < NPB)
    def _():
        lane = pl.ds(pl.multiple_of(q * BS, BS), BS)
        out[BS:, :BS] = panel[BS:, lane]

        @pl.when(dev_row > q)
        def _():
            out[:BS, :BS] = panel[:BS, lane]

        @pl.when(dev_row == q)
        def _():
            out[:BS, :BS] = upper[q].T

    @pl.when(dev_row < NPB)
    def _():
        out[:BS, BS:] = jnp.zeros((BS, 4 * BS), F32)

        @pl.when(q > dev_row)
        def _():
            out[:BS, :BS] = jnp.zeros((BS, BS), F32)


def shape(*dims):
    return jax.ShapeDtypeStruct(dims, F32)


def body(front, children, child_maps):
    col_send, col_mine, row_send, row_mine, bulk = pl.pallas_call(
        prepare_kernel,
        out_shape=[shape(5, BS, BS)] * 4 + [shape(2, 3, BS, 3 * BS)],
        in_specs=[SMEM, VMEM, VMEM],
        out_specs=[VMEM] * 5,
        name="prepare",
    )(child_maps, front, children)
    dma = pltpu.SemaphoreType.DMA
    left, right, corner = pl.pallas_call(
        spread_kernel,
        out_shape=[shape(NPB, 5, BS, BS), shape(NPB, 5, BS, BS), shape(NPB, NPB, BS, BS)],
        in_specs=[VMEM] * 4,
        out_specs=[VMEM] * 3,
        scratch_shapes=[
            pltpu.VMEM((5, BS, BS), F32),
            pltpu.VMEM((5, BS, BS), F32),
            dma((2, 5)),
            dma((2, 5)),
            dma((NPB, 5, 3)),
            dma((NPB, 5)),
            dma((NPB, 8, 4)),
            dma((NPB, 8)),
        ],
        compiler_params=pltpu.CompilerParams(collective_id=0, has_side_effects=True),
        name="spread",
    )(col_send, col_mine, row_send, row_mine)
    bulk, corner = lax.optimization_barrier((bulk, corner))
    arrived = lax.ppermute(bulk, "sub", [(0, 1), (1, 0)])
    panel, upper, base = pl.pallas_call(
        factor_kernel,
        out_shape=[shape(5 * BS, NPB * BS), shape(NPB, BS, BS), shape(5 * BS, 5 * BS)],
        in_specs=[SMEM] + [VMEM] * 5,
        out_specs=[VMEM] * 3,
        scratch_shapes=[pltpu.VMEM((NPB * BS, 5 * BS), F32)],
        cost_estimate=pl.CostEstimate(flops=10**10, bytes_accessed=10**8, transcendentals=0),
        name="factor",
    )(child_maps, corner, left, right, front, children)
    return pl.pallas_call(
        finish_kernel,
        out_shape=shape(5 * BS, 5 * BS),
        in_specs=[SMEM] + [VMEM] * 4,
        out_specs=VMEM,
        name="finish",
    )(child_maps, base, arrived, panel, upper)


def solution(mesh):
    return jax.shard_map(
        body,
        mesh=mesh,
        in_specs=(P(("sub", "row"), "col"), P("sub", "row", "col"), P()),
        out_specs=P(("sub", "row"), "col"),
        check_vma=False,
    )
```

```python
import jax
import jax.numpy as jnp
from jax import lax
from jax.experimental import pallas as pl
from jax.experimental.pallas import tpu as pltpu
from jax.sharding import PartitionSpec as P

BS = 128
NPB = 3
LEAF = 8
F32 = jnp.float32
MESH = pl.DeviceIdType.MESH
HIGHEST = lax.Precision.HIGHEST
VMEM = pl.BlockSpec(memory_space=pltpu.VMEM)
SMEM = pl.BlockSpec(memory_space=pltpu.SMEM)
ANY = pl.BlockSpec(memory_space=pl.ANY)
SOURCE = ((0, 0, 1), (2, 0, -1), (0, 1, 1))


def position():
    return lax.axis_index("sub"), lax.axis_index("row"), lax.axis_index("col")


def dot(a, b, dims):
    return lax.dot_general(a, b, (dims, ((), ())), precision=HIGHEST, preferred_element_type=F32)


def row_target(maps, child, local, row):
    return maps[child, local * 8 + row] // 16


def col_target(maps, child, m, col):
    return maps[child, m * 16 + col] // 16


def tile(ref, a, b):
    return ref.at[pl.ds(pl.multiple_of(a * BS, BS), BS), pl.ds(pl.multiple_of(b * BS, BS), BS)]


def prepare_kernel(maps, front, children, col_send, col_mine, row_send, row_mine, bulk, base):
    s, r, q = position()

    def block(c, local, m):
        return children[c, pl.ds(pl.multiple_of(local * BS, BS), BS), m * BS : (m + 1) * BS]

    @pl.when(q < NPB)
    def _():
        for n in range(5):
            col_mine[n] = front[n * BS : (n + 1) * BS, :BS]
            col_send[n] = jnp.zeros((BS, BS), F32)
        for c in range(2):
            for m in range(3):

                @pl.when(col_target(maps, 2 * s + c, m, q) == 0)
                def _():
                    for u in range(3):
                        a = row_target(maps, 2 * s + c, 2 * u + s, r)
                        col_mine[a] = col_mine[a] + block(c, 2 * u + s, m)
                        a = row_target(maps, 2 * s + c, 2 * u + 1 - s, r)
                        col_send[a] = col_send[a] + block(c, 2 * u + 1 - s, m)

    @pl.when(r < NPB)
    def _():
        for n in range(5):
            row_mine[n] = front[:BS, n * BS : (n + 1) * BS]
            row_send[n] = jnp.zeros((BS, BS), F32)
        for c in range(2):
            for u in range(3):

                @pl.when(row_target(maps, 2 * s + c, 2 * u, r) == 0)
                def _():
                    for m in range(3):
                        b = col_target(maps, 2 * s + c, m, q)

                        @pl.when(s == 0)
                        def _():
                            row_mine[b] = row_mine[b] + block(c, 2 * u, m)

                        @pl.when(s == 1)
                        def _():
                            row_send[b] = row_send[b] + block(c, 2 * u, m)

    for c in range(2):
        for u in range(3):
            bulk[c, u] = children[c, pl.ds(pl.multiple_of((2 * u + 1 - s) * BS, BS), BS), :]
    base[...] = front[...]
    for c in range(2):
        for u in range(3):
            a = row_target(maps, 2 * s + c, 2 * u + s, r)
            for m in range(3):
                t = tile(base, a, col_target(maps, 2 * s + c, m, q))
                t[...] = t[...] + block(c, 2 * u + s, m)


def eliminate_kernel(col_send, col_mine, row_send, row_mine, bulk, assembled, base, arrived,
                     left, right, corner, work, lows, inverses, uppers, panel, pr,
                     col_recv, row_recv, xs, xr, zs, zr, ys, yr, bs, br):
    s, r, q = position()
    x, y, z, core = 2 * lax.rem(r, 2) + s, r // 2, q // 2, lax.rem(q, 2)

    def at_x(d):
        nx = lax.rem(x + 4 + d, 4)
        return (lax.rem(nx, 2), 2 * y + nx // 2, q)

    def at_y(d):
        return (s, 2 * lax.rem(y + 4 + d, 4) + lax.rem(r, 2), q)

    def at_z(d):
        return (s, r, 2 * lax.rem(z + 8 + d, 8) + core)

    sibling = (s, r, 2 * z + 1 - core)
    partner = (1 - s, r, q)

    barrier = pltpu.get_barrier_semaphore()
    for peer in (at_x(1), at_x(-1), at_y(1), at_y(-1), at_z(1), at_z(-1), sibling):
        pl.semaphore_signal(barrier, inc=1, device_id=peer, device_id_type=MESH)
    pl.semaphore_wait(barrier, 7)

    def copy(src, dst, send, recv, device):
        return pltpu.make_async_remote_copy(
            src_ref=src, dst_ref=dst, send_sem=send, recv_sem=recv, device_id=device, device_id_type=MESH
        )

    def col_copy(n):
        return copy(col_send.at[n], col_recv.at[n], xs.at[0, n], xr.at[0, n], partner)

    def row_copy(n):
        return copy(row_send.at[n], row_recv.at[n], xs.at[1, n], xr.at[1, n], partner)

    col_on = q < NPB
    row_out = (r < NPB) & (s == 1)

    def bulk_copies(act):
        for c in range(2):
            for u in range(3):
                act(copy(bulk.at[c, u], arrived.at[c, u], bs.at[c, u], br.at[c, u], partner))

    def exchange(act):
        @pl.loop(0, 5)
        def _(n):
            @pl.when(col_on)
            def _():
                act(col_copy(n))

            @pl.when(row_out)
            def _():
                act(row_copy(n))

    exchange(lambda c: c.start())

    def line_place(k):
        zk, ck = k // 2, k % 2
        dz = lax.rem(z - zk + 8, 8)
        on = core == ck
        hops = jnp.where(dz <= 4, dz, 8 - dz) + jnp.where(on, 0, 1)
        return dz, on, hops

    def line_sends(k, n, act):
        dz, on, _ = line_place(k)
        here = left.at[k, n]

        @pl.when(on & (dz <= 3))
        def _():
            act(copy(here, here, zs.at[k, n, 0], zr.at[k, n], at_z(1)))

        @pl.when(on & ((dz == 0) | (dz >= 6)))
        def _():
            act(copy(here, here, zs.at[k, n, 1], zr.at[k, n], at_z(-1)))

        @pl.when(on)
        def _():
            act(copy(here, here, zs.at[k, n, 2], zr.at[k, n], sibling))

    def line_step(k, n):
        @pl.when(q == k)
        def _():
            col_copy(n).wait_recv()
            left[k, n] = col_mine[n] + col_recv[n]

        @pl.when(q != k)
        def _():
            copy(left.at[k, n], left.at[k, n], zs.at[k, n, 0], zr.at[k, n], sibling).wait_recv()

        line_sends(k, n, lambda c: c.start())

    def plane_place(i):
        xi, yi, g = SOURCE[i]
        dx, dy = lax.rem(g * (x - xi) + 4, 4), lax.rem(g * (y - yi) + 4, 4)
        hops = jnp.where(dx == 3, 1, dx) + jnp.where(dy == 3, 1, dy)
        return dx, dy, g, hops

    def plane_sends(i, here, slot, act):
        dx, dy, g, _ = plane_place(i)
        along_x = dy == 0

        @pl.when(along_x & (dx <= 1))
        def _():
            act(copy(here, here, ys.at[i, slot, 0], yr.at[i, slot], at_x(g)))

        @pl.when(along_x & (dx == 0))
        def _():
            act(copy(here, here, ys.at[i, slot, 1], yr.at[i, slot], at_x(-g)))

        @pl.when(dy <= 1)
        def _():
            act(copy(here, here, ys.at[i, slot, 2], yr.at[i, slot], at_y(g)))

        @pl.when(dy == 0)
        def _():
            act(copy(here, here, ys.at[i, slot, 3], yr.at[i, slot], at_y(-g)))

    def plane_step(i, here, slot, make):
        _, _, _, hops = plane_place(i)
        pl.when(hops == 0)(make)

        @pl.when(hops > 0)
        def _():
            copy(here, here, ys.at[i, slot, 0], yr.at[i, slot], sibling).wait_recv()

        plane_sends(i, here, slot, lambda c: c.start())

    def row_make(i, n):
        def make():
            row_copy(n).wait_recv()
            right[i, n] = row_mine[n] + row_recv[n]

        return make

    def corner_make(i, k):
        def make():
            corner[i, k] = left[k, 0]

        return make

    corners = [(i, k) for i in range(NPB) for k in range(i + 1)]

    @pl.loop(0, 10)
    def _(slot):
        for k in range(NPB):

            @pl.when(slot == line_place(k)[2])
            def _():
                line_step(k, 0)

        for i, k in corners:

            @pl.when(slot == line_place(k)[2] + plane_place(i)[3])
            def _():
                plane_step(i, corner.at[i, k], 5 + k, corner_make(i, k))

    bulk_copies(lambda c: c.start())
    for i, k in corners:
        work[i, k] = corner[i, k]

    def rest(slot):
        for k in range(NPB):
            n = slot - line_place(k)[2] + 1

            @pl.when((n >= 1) & (n < 5))
            def _():
                line_step(k, n)

        for i in range(NPB):
            n = slot - plane_place(i)[3]

            @pl.when((n >= 0) & (n < 5))
            def _():
                plane_step(i, right.at[i, n], n, row_make(i, n))

    @pl.loop(0, NPB)
    def _(k):
        def after(t):
            if t % 5 == 4:
                rest(3 * k + t // 5)

        factor_block(work.at[k, k], uppers.at[k], inverses.at[k], after)
        inv = inverses[k]
        for i in range(1, NPB):

            @pl.when(i > k)
            def _():
                lows[i, k] = dot(work[i, k], inv, ROWS_T)

        for i in range(1, NPB):
            for j in range(1, i + 1):

                @pl.when(j > k)
                def _():
                    work[i, j] = work[i, j] - dot(lows[i, k], lows[j, k], ROWS_T)

    for k in range(NPB):
        inv = inverses[k]
        mine = left[k].reshape(5 * BS, BS)
        for i in range(k):
            mine = mine - dot(panel[:, i * BS : (i + 1) * BS], lows[k, i], ROWS_T)
        panel[:, k * BS : (k + 1) * BS] = dot(mine, inv, ROWS_T)
        for n in range(5):
            other = right[k, n]
            for i in range(k):
                other = other - dot(lows[k, i], pr[i * BS : (i + 1) * BS, n * BS : (n + 1) * BS], PLAIN)
            pr[k * BS : (k + 1) * BS, n * BS : (n + 1) * BS] = dot(inv, other, PLAIN)

    for a in range(5):
        rows = slice(a * BS, (a + 1) * BS)
        base[rows, :] = assembled[rows, :] - dot(panel[rows, :], pr[...], PLAIN)

    dev_row = 8 * s + r
    for k in range(NPB):

        @pl.when(q == k)
        def _():
            base[BS:, :BS] = panel[BS:, k * BS : (k + 1) * BS]

            @pl.when(dev_row > k)
            def _():
                base[:BS, :BS] = panel[:BS, k * BS : (k + 1) * BS]

            @pl.when(dev_row == k)
            def _():
                base[:BS, :BS] = uppers[k].T

    @pl.when(dev_row < NPB)
    def _():
        base[:BS, BS:] = jnp.zeros((BS, 4 * BS), F32)

        @pl.when(q > dev_row)
        def _():
            base[:BS, :BS] = jnp.zeros((BS, BS), F32)

    bulk_copies(lambda c: c.wait())
    exchange(lambda c: c.wait_send())
    for i, k in corners:
        plane_sends(i, corner.at[i, k], 5 + k, lambda c: c.wait_send())

    @pl.loop(0, 5)
    def _(n):
        for k in range(NPB):
            line_sends(k, n, lambda c: c.wait_send())
        for i in range(NPB):
            plane_sends(i, right.at[i, n], n, lambda c: c.wait_send())


def lanes(v, j):
    return jnp.take_along_axis(v, jnp.full((8, BS), j, jnp.int32), axis=1)


def sublanes(v, i):
    return jnp.broadcast_to(v[i : i + 1, :], (8, BS))


def factor_block(block, upper, inverse, after):
    row = lax.broadcasted_iota(jnp.int32, (8, BS), 0)
    lane = lax.broadcasted_iota(jnp.int32, (8, BS), 1)
    tiles = BS // LEAF
    wa = [block[8 * t : 8 * t + 8, :] for t in range(tiles)]
    wi = [jnp.where(lane == row + 8 * t, 1.0, 0.0).astype(F32) for t in range(tiles)]
    for t in range(tiles):
        cols = {w: [lanes(wa[w], 8 * t + m) for m in range(8)] for w in range(t, tiles)}
        sc = [[sublanes(cols[t][n], m) if n <= m else None for n in range(8)] for m in range(8)]
        low = [[None] * 8 for _ in range(8)]
        rs, ua, ui = [None] * 8, [None] * 8, [None] * 8
        for m in range(8):
            rs[m] = lax.rsqrt(sc[m][m])
            for i in range(m + 1, 8):
                low[i][m] = sc[i][m] * rs[m]
            for i in range(m + 1, 8):
                for j in range(m + 1, i + 1):
                    sc[i][j] = sc[i][j] - low[i][m] * low[j][m]
            ga, gi = sublanes(wa[t], m), sublanes(wi[t], m)
            for n in range(m):
                ga = ga - low[m][n] * ua[n]
                gi = gi - low[m][n] * ui[n]
            ua[m], ui[m] = ga * rs[m], gi * rs[m]
        up, inv = ua[0], ui[0]
        for m in range(1, 8):
            up = jnp.where(row == m, ua[m], up)
            inv = jnp.where(row == m, ui[m], inv)
        upper[8 * t : 8 * t + 8, :] = jnp.where(lane >= row + 8 * t, up, 0.0)
        inverse[8 * t : 8 * t + 8, :] = jnp.where(lane <= row + 8 * t, inv, 0.0)
        after(t)
        if t == tiles - 1:
            break
        ya, yi = [None] * 8, [None] * 8
        for m in reversed(range(8)):
            a, b = ua[m], ui[m]
            for n in range(m + 1, 8):
                a = a - low[n][m] * ya[n]
                b = b - low[n][m] * yi[n]
            ya[m], yi[m] = a * rs[m], b * rs[m]
        for w in range(t + 1, tiles):
            a, b = wa[w], wi[w]
            for m in range(8):
                a = a - cols[w][m] * ya[m]
                b = b - cols[w][m] * yi[m]
            wa[w], wi[w] = a, b


ROWS_T = ((1,), (1,))
PLAIN = ((1,), (0,))


def finish_kernel(maps, base, arrived, out):
    s, r, q = position()
    out[...] = base[...]
    for c in range(2):
        child = 2 * (1 - s) + c
        for u in range(3):
            a = row_target(maps, child, 2 * u + s, r)
            for m in range(3):
                b = col_target(maps, child, m, q)
                pivot = ((a == 0) & (8 * s + r < NPB)) | ((b == 0) & (q < NPB))

                @pl.when(jnp.logical_not(pivot))
                def _():
                    t = tile(out, a, b)
                    t[...] = t[...] + arrived[c, u, :, m * BS : (m + 1) * BS]


def shape(*dims):
    return jax.ShapeDtypeStruct(dims, F32)


def body(front, children, child_maps):
    col_send, col_mine, row_send, row_mine, bulk, assembled = pl.pallas_call(
        prepare_kernel,
        out_shape=[shape(5, BS, BS)] * 4 + [shape(2, 3, BS, 3 * BS), shape(5 * BS, 5 * BS)],
        in_specs=[SMEM, VMEM, VMEM],
        out_specs=[VMEM] * 6,
        name="prepare",
    )(child_maps, front, children)
    dma = pltpu.SemaphoreType.DMA
    strips, blocks = pltpu.VMEM((NPB, 5, BS, BS), F32), pltpu.VMEM((NPB, NPB, BS, BS), F32)
    base, arrived = pl.pallas_call(
        eliminate_kernel,
        out_shape=[shape(5 * BS, 5 * BS), shape(2, 3, BS, 3 * BS)],
        in_specs=[VMEM] * 4 + [ANY, VMEM],
        out_specs=[VMEM, ANY],
        scratch_shapes=[
            strips,
            strips,
            blocks,
            blocks,
            blocks,
            pltpu.VMEM((NPB, BS, BS), F32),
            pltpu.VMEM((NPB, BS, BS), F32),
            pltpu.VMEM((5 * BS, NPB * BS), F32),
            pltpu.VMEM((NPB * BS, 5 * BS), F32),
            pltpu.VMEM((5, BS, BS), F32),
            pltpu.VMEM((5, BS, BS), F32),
            dma((2, 5)),
            dma((2, 5)),
            dma((NPB, 5, 3)),
            dma((NPB, 5)),
            dma((NPB, 8, 4)),
            dma((NPB, 8)),
            dma((2, 3)),
            dma((2, 3)),
        ],
        compiler_params=pltpu.CompilerParams(collective_id=0, has_side_effects=True),
        name="eliminate",
    )(col_send, col_mine, row_send, row_mine, bulk, assembled)
    return pl.pallas_call(
        finish_kernel,
        out_shape=shape(5 * BS, 5 * BS),
        in_specs=[SMEM, VMEM, VMEM],
        out_specs=VMEM,
        name="finish",
    )(child_maps, base, arrived)


def solution(mesh):
    return jax.shard_map(
        body,
        mesh=mesh,
        in_specs=(P(("sub", "row"), "col"), P("sub", "row", "col"), P()),
        out_specs=P(("sub", "row"), "col"),
        check_vma=False,
    )
```

```python
import jax
import jax.numpy as jnp
from jax import lax
from jax.experimental import pallas as pl
from jax.experimental.pallas import tpu as pltpu
from jax.sharding import PartitionSpec as P

BS = 128
NPB = 3
LEAF = 8
F32 = jnp.float32
MESH = pl.DeviceIdType.MESH
HIGHEST = lax.Precision.HIGHEST
VMEM = pl.BlockSpec(memory_space=pltpu.VMEM)
SMEM = pl.BlockSpec(memory_space=pltpu.SMEM)
ANY = pl.BlockSpec(memory_space=pl.ANY)
SOURCE = ((0, 0, 1), (2, 0, -1), (0, 1, 1))
HALF = BS // 2
PIECES = 12
EARLY = 4
ROW_DELAY = 3


def position():
    return lax.axis_index("sub"), lax.axis_index("row"), lax.axis_index("col")


def dot(a, b, dims):
    return lax.dot_general(a, b, (dims, ((), ())), precision=HIGHEST, preferred_element_type=F32)


def chosen(targets, want, values):
    result = jnp.zeros_like(values[0])
    for target, value in zip(targets, values):
        result = jnp.where(target == want, value, result)
    return result


def placed(rows, cols, read, down, across):
    total = {}
    for c in range(2):
        strips = [[read(c, u, m) for m in range(3)] for u in range(3)]
        for b in across:
            part = [chosen(cols[c], b, strips[u]) for u in range(3)]
            for a in down:
                value = chosen(rows[c], a, part)
                total[a, b] = total[a, b] + value if c else value
    return total


def span(start, size):
    return pl.ds(pl.multiple_of(start * size, size), size)


def lanes(v, j):
    return jnp.take_along_axis(v, jnp.full((8, BS), j, jnp.int32), axis=1)


def sublanes(v, i):
    return jnp.broadcast_to(v[i : i + 1, :], (8, BS))


def factor_block(block, upper, inverse, after):
    row = lax.broadcasted_iota(jnp.int32, (8, BS), 0)
    lane = lax.broadcasted_iota(jnp.int32, (8, BS), 1)
    tiles = BS // LEAF
    wa = [block[8 * t : 8 * t + 8, :] for t in range(tiles)]
    wi = [jnp.where(lane == row + 8 * t, 1.0, 0.0).astype(F32) for t in range(tiles)]
    for t in range(tiles):
        cols = {w: [lanes(wa[w], 8 * t + m) for m in range(8)] for w in range(t, tiles)}
        sc = [[sublanes(cols[t][n], m) if n <= m else None for n in range(8)] for m in range(8)]
        low = [[None] * 8 for _ in range(8)]
        rs, ua, ui = [None] * 8, [None] * 8, [None] * 8
        for m in range(8):
            rs[m] = lax.rsqrt(sc[m][m])
            for i in range(m + 1, 8):
                low[i][m] = sc[i][m] * rs[m]
            for i in range(m + 1, 8):
                for j in range(m + 1, i + 1):
                    sc[i][j] = sc[i][j] - low[i][m] * low[j][m]
            ga, gi = sublanes(wa[t], m), sublanes(wi[t], m)
            for n in range(m):
                ga = ga - low[m][n] * ua[n]
                gi = gi - low[m][n] * ui[n]
            ua[m], ui[m] = ga * rs[m], gi * rs[m]
        up, inv = ua[0], ui[0]
        for m in range(1, 8):
            up = jnp.where(row == m, ua[m], up)
            inv = jnp.where(row == m, ui[m], inv)
        upper[8 * t : 8 * t + 8, :] = jnp.where(lane >= row + 8 * t, up, 0.0)
        inverse[8 * t : 8 * t + 8, :] = jnp.where(lane <= row + 8 * t, inv, 0.0)
        after(t)
        if t == tiles - 1:
            break
        ya, yi = [None] * 8, [None] * 8
        for m in reversed(range(8)):
            a, b = ua[m], ui[m]
            for n in range(m + 1, 8):
                a = a - low[n][m] * ya[n]
                b = b - low[n][m] * yi[n]
            ya[m], yi[m] = a * rs[m], b * rs[m]
        for w in range(t + 1, tiles):
            a, b = wa[w], wi[w]
            for m in range(8):
                a = a - cols[w][m] * ya[m]
                b = b - cols[w][m] * yi[m]
            wa[w], wi[w] = a, b


ROWS_T = ((1,), (1,))
PLAIN = ((1,), (0,))


def kernel(maps, front, children, out, kids, arrived, left, right, corner, work, lows, inverses, uppers, panel, pr,
           col_send, col_mine, col_recv, row_send, row_mine, row_recv,
           fs, xs, xr, zs, zr, ys, yr, ls, cx, cy, cb, cr, br, ps, pq):
    s, r, q = position()
    dev_row = 8 * s + r
    x, y, z, core = 2 * lax.rem(r, 2) + s, r // 2, q // 2, lax.rem(q, 2)

    def at_x(d):
        nx = lax.rem(x + 4 + d, 4)
        return (lax.rem(nx, 2), 2 * y + nx // 2, q)

    def at_y(d):
        return (s, 2 * lax.rem(y + 4 + d, 4) + lax.rem(r, 2), q)

    def at_z(d, to_core=core):
        return (s, r, 2 * lax.rem(z + 8 + d, 8) + to_core)

    sibling = (s, r, 2 * z + 1 - core)
    partner = (1 - s, r, q)

    barrier = pltpu.get_barrier_semaphore()
    peers = [at_x(d) for d in (1, 2, 3)] + [at_y(d) for d in (1, 2, 3)]
    peers += [at_z(d, c) for d in range(1, 8) for c in range(2)] + [sibling]
    for peer in peers:
        pl.semaphore_signal(barrier, inc=1, device_id=peer, device_id_type=MESH)
    fetch = [pltpu.make_async_copy(children.at[c], kids.at[c], fs.at[c]) for c in range(2)]
    fetch.append(pltpu.make_async_copy(front, out, fs.at[2]))
    for f in fetch:
        f.start()

    def copy(src, dst, send, recv, device):
        return pltpu.make_async_remote_copy(
            src_ref=src, dst_ref=dst, send_sem=send, recv_sem=recv, device_id=device, device_id_type=MESH
        )

    def rows_of(child, side):
        return [maps[child, (2 * u + side) * 8 + r] // 16 for u in range(3)]

    def cols_of(child):
        return [maps[child, m * 16 + q] // 16 for m in range(3)]

    mine = [(2 * s + c) for c in range(2)]
    cols = [cols_of(child) for child in mine]
    kept = [rows_of(child, s) for child in mine]
    given = [rows_of(child, 1 - s) for child in mine]

    def strips(body):
        @pl.loop(0, BS // 8)
        def _(i):
            body(lambda a: pl.ds(pl.multiple_of(a * BS + 8 * i, 8), 8))

    def own(at, side):
        return lambda c, u, m: kids[c, at(2 * u + side), m * BS : (m + 1) * BS]

    for f in fetch:
        f.wait()

    @pl.when(q < NPB)
    def _():
        @strips
        def _(at):
            sent = placed(given, cols, own(at, 1 - s), range(5), [0])
            stay = placed(kept, cols, own(at, s), range(5), [0])
            for n in range(5):
                col_send[n, at(0), :] = sent[n, 0]
                col_mine[n, at(0), :] = out[at(n), :BS] + stay[n, 0]

    @pl.when(r < NPB)
    def _():
        @strips
        def _(at):
            first = placed([rows_of(child, 0) for child in mine], cols, own(at, 0), [0], range(5))
            for n in range(5):
                row_send[n, at(0), :] = first[0, n]
                row_mine[n, at(0), :] = out[at(0), n * BS : (n + 1) * BS] + first[0, n]

    pl.semaphore_wait(barrier, len(peers))

    def col_copy(n):
        return copy(col_send.at[n], col_recv.at[n], xs.at[0, n], xr.at[0, n], partner)

    def row_copy(n):
        return copy(row_send.at[n], row_recv.at[n], xs.at[1, n], xr.at[1, n], partner)

    def exchange(act):
        @pl.when(q < NPB)
        def _():
            for n in range(5):
                act(col_copy(n))

        @pl.when((r < NPB) & (s == 1))
        def _():
            for n in range(5):
                act(row_copy(n))

    def piece(j):
        c, u, half = j // 6, lax.rem(j // 2, 3), lax.rem(j, 2)
        return copy(
            kids.at[c, pl.ds(pl.multiple_of((2 * u + 1 - s) * BS + half * HALF, HALF), HALF), :],
            arrived.at[c, u, pl.ds(pl.multiple_of(half * HALF, HALF), HALF), :],
            ps.at[j], pq.at[j], partner,
        )

    patient = (s == 0) & (y < 2)
    exchange(lambda c: c.start())

    @pl.when(jnp.logical_not(patient))
    def _():
        @pl.loop(0, PIECES)
        def _(j):
            piece(j).start()

    def add(rows, cols, read):
        @strips
        def _(at):
            total = placed(rows, cols, read(at), range(5), range(5))
            for a in range(5):
                for b in range(5):
                    lanes_b = slice(b * BS, (b + 1) * BS)
                    out[at(a), lanes_b] = out[at(a), lanes_b] + total[a, b]

    add(kept, cols, lambda at: own(at, s))

    line = []
    for k in range(NPB):
        dz = lax.rem(z - k // 2 + 8, 8)
        on = core == k % 2
        hops = jnp.where(dz <= 4, dz, 8 - dz) + jnp.where(on, 0, 1)
        line.append((on & (dz <= 3), on & ((dz == 0) | (dz >= 6)), on, hops))
    z_up, z_down = at_z(1), at_z(-1)

    def line_sends(k, n, act):
        up, down, on, _ = line[k]
        here = left.at[k, n]

        @pl.when(up)
        def _():
            act(copy(here, here, zs.at[k, n, 0], zr.at[k, n], z_up))

        @pl.when(down)
        def _():
            act(copy(here, here, zs.at[k, n, 1], zr.at[k, n], z_down))

        @pl.when(on)
        def _():
            act(copy(here, here, zs.at[k, n, 2], zr.at[k, n], sibling))

    def col_make(k, n):
        col_copy(n).wait_recv()
        left[k, n] = col_mine[n] + col_recv[n]

    def line_step(k, n):
        @pl.when((q == k) & (n > 0))
        def _():
            col_make(k, n)

        @pl.when(q != k)
        def _():
            copy(left.at[k, n], left.at[k, n], zs.at[k, n, 0], zr.at[k, n], sibling).wait_recv()

        line_sends(k, n, lambda c: c.start())

    plane = []
    for xi, yi, g in SOURCE:
        dx, dy = lax.rem(x - xi + 4, 4), lax.rem(g * (y - yi) + 4, 4)
        hops = jnp.where(dx == 3, 1, dx) + jnp.where(dy == 3, 1, dy)
        plane.append(((dy == 0) & (dx <= 1), (dy == 0) & (dx == 0), dy <= 1, dy == 0, hops))
    x_up, x_down, y_up, y_down = at_x(1), at_x(-1), at_y(1), at_y(-1)

    def plane_sends(i, n, act):
        g = SOURCE[i][2]
        here = right.at[i, n]
        targets = (x_up, x_down, y_up if g > 0 else y_down, y_down if g > 0 else y_up)
        for way in range(4):

            @pl.when(plane[i][way])
            def _():
                act(copy(here, here, ys.at[i, n, way], yr.at[i, n], targets[way]))

    def plane_step(i, n):
        @pl.when(plane[i][4] == 0)
        def _():
            row_copy(n).wait_recv()
            right[i, n] = row_mine[n] + row_recv[n]

        @pl.when(plane[i][4] > 0)
        def _():
            copy(right.at[i, n], right.at[i, n], ys.at[i, n, 0], yr.at[i, n], sibling).wait_recv()

        plane_sends(i, n, lambda c: c.start())

    corners = [(i, k) for i in range(NPB) for k in range(i + 1)]
    my_half = span(core, HALF)
    far_z = (4, 3, 5, 2, 6, 1, 7)

    def corner_stage(i):
        xi, yi, _ = SOURCE[i]
        at_line = dev_row == i
        return at_line, y == yi

    def corner_line(i, k, act):
        for d in range(7):
            for c in range(2):
                part = corner.at[i, k, c * HALF : (c + 1) * HALF, :]
                act(copy(part, part, ls.at[2 * d + c], cr.at[i, k], at_z(far_z[d], c)))
        part = corner.at[i, k, span(1 - core, HALF), :]
        act(copy(part, part, ls.at[14], cr.at[i, k], sibling))

    def corner_sends(i, k, act):
        at_line, at_row = corner_stage(i)
        part = corner.at[i, k, my_half, :]

        @pl.when(at_line & (q == k))
        def _():
            corner_line(i, k, act)

        @pl.when(at_line)
        def _():
            for d in (2, 1, 3):
                act(copy(part, part, cx.at[i, k, d], cr.at[i, k], at_x(d)))

        @pl.when(at_row)
        def _():
            for d in (2, 1, 3):
                act(copy(part, part, cy.at[i, k, d], cr.at[i, k], at_y(d)))

        @pl.when(jnp.logical_not(at_line & (q == k ^ 1)))
        def _():
            act(copy(part, part, cb.at[i, k], br.at[i, k], sibling))

    def corner_step(i, k, stage):
        at_line, at_row = corner_stage(i)
        mine_now = (at_line & (q == k), at_line & (q != k), at_row & jnp.logical_not(at_line), jnp.logical_not(at_row))

        @pl.when(mine_now[stage])
        def _():
            if stage == 0:
                corner[i, k] = left[k, 0]
            else:
                part = corner.at[i, k, my_half, :]
                copy(part, part, cb.at[i, k], cr.at[i, k], sibling).wait_recv()
            corner_sends(i, k, lambda c: c.start())

    for k in range(NPB):

        @pl.when(q == k)
        def _():
            col_make(k, 0)

    def rest(slot):
        for k in range(NPB):
            n = slot - line[k][3]

            @pl.when((n >= 0) & (n < 5))
            def _():
                line_step(k, n)

        for i in range(NPB):
            n = slot - plane[i][4] - ROW_DELAY

            @pl.when((n >= 0) & (n < 5))
            def _():
                plane_step(i, n)

        if isinstance(slot, int) and slot < ROW_DELAY:
            return

        @pl.when(patient)
        def _():
            piece(slot - ROW_DELAY).start()

    for slot in range(EARLY):
        for i, k in corners:
            corner_step(i, k, slot)
        rest(slot)
    for i, k in corners:
        other = corner.at[i, k, span(1 - core, HALF), :]

        @pl.when(jnp.logical_not((dev_row == i) & (q == k)))
        def _():
            copy(other, other, cb.at[i, k], br.at[i, k], sibling).wait_recv()

        work[i, k] = corner[i, k]

    @pl.loop(0, NPB)
    def _(k):
        def after(t):
            if t % 5 == 4:
                rest(EARLY + 3 * k + t // 5)

        factor_block(work.at[k, k], uppers.at[k], inverses.at[k], after)
        inv = inverses[k]
        for i in range(1, NPB):

            @pl.when(i > k)
            def _():
                lows[i, k] = dot(work[i, k], inv, ROWS_T)

        for i in range(1, NPB):
            for j in range(1, i + 1):

                @pl.when(j > k)
                def _():
                    work[i, j] = work[i, j] - dot(lows[i, k], lows[j, k], ROWS_T)

    @pl.loop(EARLY + 9, ROW_DELAY + PIECES)
    def _(slot):
        rest(slot)

    for k in range(NPB):
        inv = inverses[k]
        own = left[k].reshape(5 * BS, BS)
        for i in range(k):
            own = own - dot(panel[:, i * BS : (i + 1) * BS], lows[k, i], ROWS_T)
        panel[:, k * BS : (k + 1) * BS] = dot(own, inv, ROWS_T)
        for n in range(5):
            other = right[k, n]
            for i in range(k):
                other = other - dot(lows[k, i], pr[i * BS : (i + 1) * BS, n * BS : (n + 1) * BS], PLAIN)
            pr[k * BS : (k + 1) * BS, n * BS : (n + 1) * BS] = dot(inv, other, PLAIN)

    for a in range(5):
        rows = slice(a * BS, (a + 1) * BS)
        out[rows, :] = out[rows, :] - dot(panel[rows, :], pr[...], PLAIN)

    @pl.loop(0, PIECES)
    def _(j):
        piece(j).wait()

    theirs = [2 * (1 - s) + c for c in range(2)]
    add(
        [rows_of(child, s) for child in theirs],
        [cols_of(child) for child in theirs],
        lambda at: lambda c, u, m: arrived[c, u, at(0), m * BS : (m + 1) * BS],
    )

    for k in range(NPB):

        @pl.when(q == k)
        def _():
            out[BS:, :BS] = panel[BS:, k * BS : (k + 1) * BS]

            @pl.when(dev_row > k)
            def _():
                out[:BS, :BS] = panel[:BS, k * BS : (k + 1) * BS]

            @pl.when(dev_row == k)
            def _():
                out[:BS, :BS] = uppers[k].T

    @pl.when(dev_row < NPB)
    def _():
        out[:BS, BS:] = jnp.zeros((BS, 4 * BS), F32)

        @pl.when(q > dev_row)
        def _():
            out[:BS, :BS] = jnp.zeros((BS, BS), F32)

    exchange(lambda c: c.wait_send())
    for i, k in corners:
        corner_sends(i, k, lambda c: c.wait_send())

    @pl.loop(0, 5)
    def _(n):
        for k in range(NPB):
            line_sends(k, n, lambda c: c.wait_send())
        for i in range(NPB):
            plane_sends(i, n, lambda c: c.wait_send())


def body(front, children, child_maps):
    dma = pltpu.SemaphoreType.DMA

    def vmem(*dims):
        return pltpu.VMEM(dims, F32)

    return pl.pallas_call(
        kernel,
        out_shape=jax.ShapeDtypeStruct((5 * BS, 5 * BS), F32),
        in_specs=[SMEM, ANY, ANY],
        out_specs=VMEM,
        scratch_shapes=[
            vmem(2, 6 * BS, 3 * BS),
            vmem(2, 3, BS, 3 * BS),
            vmem(NPB, 5, BS, BS),
            vmem(NPB, 5, BS, BS),
            vmem(NPB, NPB, BS, BS),
            vmem(NPB, NPB, BS, BS),
            vmem(NPB, NPB, BS, BS),
            vmem(NPB, BS, BS),
            vmem(NPB, BS, BS),
            vmem(5 * BS, NPB * BS),
            vmem(NPB * BS, 5 * BS),
        ]
        + [vmem(5, BS, BS)] * 6
        + [
            dma((3,)),
            dma((2, 5)),
            dma((2, 5)),
            dma((NPB, 5, 3)),
            dma((NPB, 5)),
            dma((NPB, 5, 4)),
            dma((NPB, 5)),
            dma((15,)),
            dma((NPB, NPB, 4)),
            dma((NPB, NPB, 4)),
            dma((NPB, NPB)),
            dma((NPB, NPB)),
            dma((NPB, NPB)),
            dma((PIECES,)),
            dma((PIECES,)),
        ],
        compiler_params=pltpu.CompilerParams(collective_id=0, has_side_effects=True),
        name="front",
    )(child_maps, front, children)


def solution(mesh):
    return jax.shard_map(
        body,
        mesh=mesh,
        in_specs=(P(("sub", "row"), "col"), P("sub", "row", "col"), P()),
        out_specs=P(("sub", "row"), "col"),
        check_vma=False,
    )
```

```python
import jax
import jax.numpy as jnp
from jax import lax
from jax.experimental import pallas as pl
from jax.experimental.pallas import tpu as pltpu
from jax.sharding import PartitionSpec as P

BS = 128
NPB = 3
LEAF = 8
Y_AT = (0, 4)
Z_AT = (1, 4)
F32 = jnp.float32
MESH = pl.DeviceIdType.MESH
HIGHEST = lax.Precision.HIGHEST
VMEM = pl.BlockSpec(memory_space=pltpu.VMEM)
SMEM = pl.BlockSpec(memory_space=pltpu.SMEM)
ANY = pl.BlockSpec(memory_space=pl.ANY)
SOURCE = ((0, 0), (2, 0), (0, 1))
HALF = BS // 2


def position():
    return lax.axis_index("sub"), lax.axis_index("row"), lax.axis_index("col")


def dot(a, b, dims):
    return lax.dot_general(a, b, (dims, ((), ())), precision=HIGHEST, preferred_element_type=F32)


def chosen(targets, want, values):
    result = jnp.zeros_like(values[0])
    for target, value in zip(targets, values):
        result = jnp.where(target == want, value, result)
    return result


def placed(rows, cols, read, down, across):
    total = {}
    for c in range(2):
        strips = [[read(c, u, m) for m in range(3)] for u in range(3)]
        for b in across:
            part = [chosen(cols[c], b, strips[u]) for u in range(3)]
            for a in down:
                value = chosen(rows[c], a, part)
                total[a, b] = total[a, b] + value if c else value
    return total


def span(start, size):
    return pl.ds(pl.multiple_of(start * size, size), size)


def lanes(v, j):
    return jnp.take_along_axis(v, jnp.full((8, BS), j, jnp.int32), axis=1)


def sublanes(v, i):
    return jnp.broadcast_to(v[i : i + 1, :], (8, BS))


def factor_block(block, upper, inverse, after):
    row = lax.broadcasted_iota(jnp.int32, (8, BS), 0)
    lane = lax.broadcasted_iota(jnp.int32, (8, BS), 1)
    tiles = BS // LEAF
    wa = [block[8 * t : 8 * t + 8, :] for t in range(tiles)]
    wi = [jnp.where(lane == row + 8 * t, 1.0, 0.0).astype(F32) for t in range(tiles)]
    for t in range(tiles):
        cols = {w: [lanes(wa[w], 8 * t + m) for m in range(8)] for w in range(t, tiles)}
        sc = [[sublanes(cols[t][n], m) if n <= m else None for n in range(8)] for m in range(8)]
        low = [[None] * 8 for _ in range(8)]
        rs, ua, ui = [None] * 8, [None] * 8, [None] * 8
        for m in range(8):
            rs[m] = lax.rsqrt(sc[m][m])
            for i in range(m + 1, 8):
                low[i][m] = sc[i][m] * rs[m]
            for i in range(m + 1, 8):
                for j in range(m + 1, i + 1):
                    sc[i][j] = sc[i][j] - low[i][m] * low[j][m]
            ga, gi = sublanes(wa[t], m), sublanes(wi[t], m)
            for n in range(m):
                ga = ga - low[m][n] * ua[n]
                gi = gi - low[m][n] * ui[n]
            ua[m], ui[m] = ga * rs[m], gi * rs[m]
        up, inv = ua[0], ui[0]
        for m in range(1, 8):
            up = jnp.where(row == m, ua[m], up)
            inv = jnp.where(row == m, ui[m], inv)
        upper[8 * t : 8 * t + 8, :] = jnp.where(lane >= row + 8 * t, up, 0.0)
        inverse[8 * t : 8 * t + 8, :] = jnp.where(lane <= row + 8 * t, inv, 0.0)
        after(t)
        if t == tiles - 1:
            break
        ya, yi = [None] * 8, [None] * 8
        for m in reversed(range(8)):
            a, b = ua[m], ui[m]
            for n in range(m + 1, 8):
                a = a - low[n][m] * ya[n]
                b = b - low[n][m] * yi[n]
            ya[m], yi[m] = a * rs[m], b * rs[m]
        for w in range(t + 1, tiles):
            a, b = wa[w], wi[w]
            for m in range(8):
                a = a - cols[w][m] * ya[m]
                b = b - cols[w][m] * yi[m]
            wa[w], wi[w] = a, b


ROWS_T = ((1,), (1,))
PLAIN = ((1,), (0,))


def kernel(maps, front, children, out, kids, arrived, left, right, corner, work, lows, inverses, uppers, panel, pr,
           col_send, col_mine, row_send, row_mine, first_recv, line_in, plane_in,
           fs, xs, sl, sp, rl, rp, gs, gr, hs, hr, ws, wr, bs, br, ls, cx, cy, cb, cr, cbr, ps, pq):
    s, r, q = position()
    dev_row = 8 * s + r
    x, y, z, core = 2 * lax.rem(r, 2) + s, r // 2, q // 2, lax.rem(q, 2)

    def at_x(d):
        nx = lax.rem(x + 4 + d, 4)
        return (lax.rem(nx, 2), 2 * y + nx // 2, q)

    def at_y(d):
        return (s, 2 * lax.rem(y + 4 + d, 4) + lax.rem(r, 2), q)

    def at_z(d, to_core=core):
        return (s, r, 2 * lax.rem(z + 8 + d, 8) + to_core)

    sibling = (s, r, 2 * z + 1 - core)
    partner = (1 - s, r, q)

    barrier = pltpu.get_barrier_semaphore()
    plane_peers = [(dx, dy) for dx in range(4) for dy in range(4)]
    line_peers = [(dz, c) for dz in range(8) for c in range(2)]

    def in_line(side, dz, c):
        return (side, r, 2 * lax.rem(z + dz, 8) + lax.rem(core + c, 2))

    def in_plane(dx, dy):
        nx = lax.rem(x + dx, 4)
        return (lax.rem(nx, 2), 2 * lax.rem(y + dy, 4) + nx // 2, q)

    peers = [in_line(s, *p) for p in line_peers[1:]] + [in_line(1 - s, *p) for p in line_peers[1:]]
    peers += [in_plane(*p) for p in plane_peers[1:]]
    for peer in peers:
        pl.semaphore_signal(barrier, inc=1, device_id=peer, device_id_type=MESH)
    fetch = [pltpu.make_async_copy(children.at[c], kids.at[c], fs.at[c]) for c in range(2)]
    fetch.append(pltpu.make_async_copy(front, out, fs.at[2]))
    for f in fetch:
        f.start()

    def copy(src, dst, send, recv, device):
        return pltpu.make_async_remote_copy(
            src_ref=src, dst_ref=dst, send_sem=send, recv_sem=recv, device_id=device, device_id_type=MESH
        )

    def rows_of(child, side):
        return [maps[child, (2 * u + side) * 8 + r] // 16 for u in range(3)]

    def cols_of(child):
        return [maps[child, m * 16 + q] // 16 for m in range(3)]

    mine = [(2 * s + c) for c in range(2)]
    cols = [cols_of(child) for child in mine]
    kept = [rows_of(child, s) for child in mine]
    given = [rows_of(child, 1 - s) for child in mine]

    def strips(body):
        @pl.loop(0, BS // 8)
        def _(i):
            body(lambda a: pl.ds(pl.multiple_of(a * BS + 8 * i, 8), 8))

    def own(at, side):
        return lambda c, u, m: kids[c, at(2 * u + side), m * BS : (m + 1) * BS]

    for f in fetch:
        f.wait()

    @pl.when(q < NPB)
    def _():
        @strips
        def _(at):
            sent = placed(given, cols, own(at, 1 - s), range(5), [0])
            stay = placed(kept, cols, own(at, s), range(5), [0])
            for n in range(5):
                col_send[n, at(0), :] = sent[n, 0]
                col_mine[n, at(0), :] = out[at(n), :BS] + stay[n, 0]

    @pl.when(r < NPB)
    def _():
        @strips
        def _(at):
            first = placed([rows_of(child, 0) for child in mine], cols, own(at, 0), [0], range(5))
            for n in range(5):
                row_send[n, at(0), :] = first[0, n]
                row_mine[n, at(0), :] = out[at(0), n * BS : (n + 1) * BS] + first[0, n]

    pl.semaphore_wait(barrier, len(peers))

    def first_copy():
        return copy(col_send.at[0], first_recv, xs.at[0], xs.at[1], partner)

    first_on = (r < NPB) & (q < NPB)

    @pl.when(first_on & (s == 1))
    def _():
        first_copy().start()

    def line_rows(dz, c):
        return pl.ds(pl.multiple_of(HALF * lax.rem(core + c, 2) + 8 * lax.rem(z + dz, 8), 8), 8)

    def plane_rows(dx, dy):
        return pl.ds(pl.multiple_of(32 * lax.rem(y + dy, 4) + 8 * lax.rem(x + dx, 4), 8), 8)

    own_line, own_plane = line_rows(0, 0), plane_rows(0, 0)

    def scatter(act):
        for k in range(NPB):

            @pl.when(q == k)
            def _():
                for j, p in enumerate(line_peers):
                    rows = line_rows(*p)
                    act(copy(col_send.at[:, rows], line_in.at[k, 1], sl.at[1, j], rl.at[k, 1], in_line(1 - s, *p)))
                    if j:
                        act(copy(col_mine.at[:, rows], line_in.at[k, 0], sl.at[0, j], rl.at[k, 0], in_line(s, *p)))

        for i in range(NPB):
            for side, held in ((0, row_mine), (1, row_send)):

                @pl.when((r == i) & (s == side))
                def _():
                    for j, p in enumerate(plane_peers):
                        if j:
                            rows = plane_rows(*p)
                            act(copy(held.at[:, rows], plane_in.at[i, side], sp.at[j], rp.at[i, side], in_plane(*p)))

    def gather_sum():
        for k in range(NPB):
            copy(line_in.at[k, 1], line_in.at[k, 1], sl.at[1, 0], rl.at[k, 1], sibling).wait_recv()

            @pl.when(q == k)
            def _():
                left[k, :, own_line, :] = col_mine[:, own_line, :] + line_in[k, 1]

            @pl.when(q != k)
            def _():
                copy(line_in.at[k, 0], line_in.at[k, 0], sl.at[0, 0], rl.at[k, 0], sibling).wait_recv()
                left[k, :, own_line, :] = line_in[k, 0] + line_in[k, 1]

        for i in range(NPB):
            for side, held in ((0, row_mine), (1, row_send)):
                holder = (r == i) & (s == side)

                @pl.when(holder)
                def _():
                    plane_in[i, side] = held[:, own_plane, :]

                @pl.when(jnp.logical_not(holder))
                def _():
                    copy(plane_in.at[i, side], plane_in.at[i, side], sp.at[0], rp.at[i, side], sibling).wait_recv()

            right[i, :, own_plane, :] = plane_in[i, 0] + plane_in[i, 1]

    def along_z(act):
        here = left.at[:, :, own_line]
        for d in (4, 3, 5, 2, 6, 1, 7):
            act(copy(here, here, gs.at[d], gr.at[d], at_z(d)))

    def along_x(act):
        here = right.at[:, :, own_plane]
        for d in (2, 1, 3):
            act(copy(here, here, hs.at[d], hr.at[d], at_x(d)))

    def along_y(act):
        here = right.at[:, :, span(y, 32)]
        for d in (2, 1, 3):
            act(copy(here, here, ws.at[d], wr.at[d], at_y(d)))

    def to_sibling(act):
        here = left.at[:, :, span(core, HALF)]
        act(copy(here, here, bs.at[0], br.at[0], sibling))

    def pieces(act):
        for c in range(2):
            for u in range(3):
                act(copy(kids.at[c, span(2 * u + 1 - s, BS), :], arrived.at[c, u], ps.at[c, u], pq.at[c, u], partner))

    def add(rows, cols, read):
        @strips
        def _(at):
            total = placed(rows, cols, read(at), range(5), range(5))
            for a in range(5):
                for b in range(5):
                    lanes_b = slice(b * BS, (b + 1) * BS)
                    out[at(a), lanes_b] = out[at(a), lanes_b] + total[a, b]

    add(kept, cols, lambda at: own(at, s))

    corners = [(i, k) for i in range(NPB) for k in range(i + 1)]
    my_half = span(core, HALF)
    far_z = (4, 3, 5, 2, 6, 1, 7)

    def corner_stage(i):
        _, yi = SOURCE[i]
        at_line = dev_row == i
        return at_line, y == yi

    def corner_line(i, k, act):
        for d in range(7):
            for c in range(2):
                part = corner.at[i, k, c * HALF : (c + 1) * HALF, :]
                act(copy(part, part, ls.at[2 * d + c], cr.at[i, k], at_z(far_z[d], c)))
        part = corner.at[i, k, span(1 - core, HALF), :]
        act(copy(part, part, ls.at[14], cr.at[i, k], sibling))

    def corner_sends(i, k, act):
        at_line, at_row = corner_stage(i)
        part = corner.at[i, k, my_half, :]

        @pl.when(at_line & (q == k))
        def _():
            corner_line(i, k, act)

        @pl.when(at_line)
        def _():
            for d in (2, 1, 3):
                act(copy(part, part, cx.at[i, k, d], cr.at[i, k], at_x(d)))

        @pl.when(at_row)
        def _():
            for d in (2, 1, 3):
                act(copy(part, part, cy.at[i, k, d], cr.at[i, k], at_y(d)))

        @pl.when(jnp.logical_not(at_line & (q == k ^ 1)))
        def _():
            act(copy(part, part, cb.at[i, k], cbr.at[i, k], sibling))

    def corner_step(i, k, stage):
        at_line, at_row = corner_stage(i)
        mine_now = (at_line & (q == k), at_line & (q != k), at_row & jnp.logical_not(at_line), jnp.logical_not(at_row))

        @pl.when(mine_now[stage])
        def _():
            if stage == 0:
                first_copy().wait_recv()
                corner[i, k] = col_mine[0] + first_recv[...]
            else:
                part = corner.at[i, k, my_half, :]
                copy(part, part, cb.at[i, k], cr.at[i, k], sibling).wait_recv()
            corner_sends(i, k, lambda c: c.start())

    @pl.when(first_on & (s == 0) & (q > r))
    def _():
        first_copy().wait_recv()

    for stage in range(4):
        for i, k in corners:
            corner_step(i, k, stage)
        if stage == 0:
            scatter(lambda c: c.start())
    gather_sum()
    along_x(lambda c: c.start())
    along_z(lambda c: c.start())
    pieces(lambda c: c.start())
    for i, k in corners:
        other = corner.at[i, k, span(1 - core, HALF), :]

        @pl.when(jnp.logical_not((dev_row == i) & (q == k)))
        def _():
            copy(other, other, cb.at[i, k], cbr.at[i, k], sibling).wait_recv()

        work[i, k] = corner[i, k]

    @pl.loop(0, NPB)
    def _(k):
        def after(t):
            if t == Y_AT[1]:

                @pl.when(k == Y_AT[0])
                def _():
                    along_x(lambda c: c.wait_recv())
                    along_y(lambda c: c.start())

            if t == Z_AT[1]:

                @pl.when(k == Z_AT[0])
                def _():
                    along_z(lambda c: c.wait_recv())
                    to_sibling(lambda c: c.start())

        factor_block(work.at[k, k], uppers.at[k], inverses.at[k], after)
        inv = inverses[k]
        for i in range(1, NPB):

            @pl.when(i > k)
            def _():
                lows[i, k] = dot(work[i, k], inv, ROWS_T)

        for i in range(1, NPB):
            for j in range(1, i + 1):

                @pl.when(j > k)
                def _():
                    work[i, j] = work[i, j] - dot(lows[i, k], lows[j, k], ROWS_T)

    along_y(lambda c: c.wait_recv())
    to_sibling(lambda c: c.wait_recv())

    for k in range(NPB):
        inv = inverses[k]
        own = left[k].reshape(5 * BS, BS)
        for i in range(k):
            own = own - dot(panel[:, i * BS : (i + 1) * BS], lows[k, i], ROWS_T)
        panel[:, k * BS : (k + 1) * BS] = dot(own, inv, ROWS_T)
        for n in range(5):
            other = right[k, n]
            for i in range(k):
                other = other - dot(lows[k, i], pr[i * BS : (i + 1) * BS, n * BS : (n + 1) * BS], PLAIN)
            pr[k * BS : (k + 1) * BS, n * BS : (n + 1) * BS] = dot(inv, other, PLAIN)

    for a in range(5):
        rows = slice(a * BS, (a + 1) * BS)
        out[rows, :] = out[rows, :] - dot(panel[rows, :], pr[...], PLAIN)

    pieces(lambda c: c.wait())

    theirs = [2 * (1 - s) + c for c in range(2)]
    add(
        [rows_of(child, s) for child in theirs],
        [cols_of(child) for child in theirs],
        lambda at: lambda c, u, m: arrived[c, u, at(0), m * BS : (m + 1) * BS],
    )

    for k in range(NPB):

        @pl.when(q == k)
        def _():
            out[BS:, :BS] = panel[BS:, k * BS : (k + 1) * BS]

            @pl.when(dev_row > k)
            def _():
                out[:BS, :BS] = panel[:BS, k * BS : (k + 1) * BS]

            @pl.when(dev_row == k)
            def _():
                out[:BS, :BS] = uppers[k].T

    @pl.when(first_on & (s == 1))
    def _():
        first_copy().wait_send()

    scatter(lambda c: c.wait_send())
    for act in (along_x, along_y, along_z, to_sibling):
        act(lambda c: c.wait_send())
    for i, k in corners:
        corner_sends(i, k, lambda c: c.wait_send())


def body(front, children, child_maps):
    dma = pltpu.SemaphoreType.DMA

    def vmem(*dims):
        return pltpu.VMEM(dims, F32)

    done = pl.pallas_call(
        kernel,
        out_shape=jax.ShapeDtypeStruct((5 * BS, 5 * BS), F32),
        in_specs=[SMEM, ANY, ANY],
        out_specs=VMEM,
        scratch_shapes=[
            vmem(2, 6 * BS, 3 * BS),
            vmem(2, 3, BS, 3 * BS),
            vmem(NPB, 5, BS, BS),
            vmem(NPB, 5, BS, BS),
            vmem(NPB, NPB, BS, BS),
            vmem(NPB, NPB, BS, BS),
            vmem(NPB, NPB, BS, BS),
            vmem(NPB, BS, BS),
            vmem(NPB, BS, BS),
            vmem(5 * BS, NPB * BS),
            vmem(NPB * BS, 5 * BS),
        ]
        + [vmem(5, BS, BS)] * 4
        + [vmem(BS, BS), vmem(NPB, 2, 5, 8, BS), vmem(NPB, 2, 5, 8, BS)]
        + [
            dma((3,)),
            dma((2,)),
            dma((2, 16)),
            dma((16,)),
            dma((NPB, 2)),
            dma((NPB, 2)),
            dma((8,)),
            dma((8,)),
            dma((4,)),
            dma((4,)),
            dma((4,)),
            dma((4,)),
            dma((1,)),
            dma((1,)),
            dma((15,)),
            dma((NPB, NPB, 4)),
            dma((NPB, NPB, 4)),
            dma((NPB, NPB)),
            dma((NPB, NPB)),
            dma((NPB, NPB)),
            dma((2, 3)),
            dma((2, 3)),
        ],
        compiler_params=pltpu.CompilerParams(collective_id=0, has_side_effects=True),
        name="front",
    )(child_maps, front, children)
    s, r, q = position()
    section = 8 * s + r
    row = lax.broadcasted_iota(jnp.int32, done.shape, 0)
    column = lax.broadcasted_iota(jnp.int32, done.shape, 1)
    return jnp.where((section < NPB) & (row < BS) & (column // BS * 16 + q > section), 0.0, done)


def solution(mesh):
    return jax.shard_map(
        body,
        mesh=mesh,
        in_specs=(P(("sub", "row"), "col"), P("sub", "row", "col"), P()),
        out_specs=P(("sub", "row"), "col"),
        check_vma=False,
    )
```

```python
import jax
import jax.numpy as jnp
from jax import lax
from jax.experimental import pallas as pl
from jax.experimental.pallas import tpu as pltpu
from jax.sharding import PartitionSpec as P

BS = 128
NPB = 3
LEAF = 8
SUM_AFTER = 1
Y_AT = (0, 4)
Z_AT = (1, 4)
F32 = jnp.float32
MESH = pl.DeviceIdType.MESH
HIGHEST = lax.Precision.HIGHEST
VMEM = pl.BlockSpec(memory_space=pltpu.VMEM)
SMEM = pl.BlockSpec(memory_space=pltpu.SMEM)
ANY = pl.BlockSpec(memory_space=pl.ANY)
SOURCE = ((0, 0), (2, 0), (0, 1))
HALF = BS // 2


def position():
    return lax.axis_index("sub"), lax.axis_index("row"), lax.axis_index("col")


def split(a):
    high = a.astype(jnp.bfloat16)
    return high, (a - high.astype(F32)).astype(jnp.bfloat16)


def dot3(a, b, dims):
    def part(u, v):
        return lax.dot_general(u, v, (dims, ((), ())), preferred_element_type=F32)

    return part(a[0], b[0]) + (part(a[0], b[1]) + part(a[1], b[0]))


def dot(a, b, dims):
    return lax.dot_general(a, b, (dims, ((), ())), precision=HIGHEST, preferred_element_type=F32)


def chosen(targets, want, values):
    result = jnp.zeros_like(values[0])
    for target, value in zip(targets, values):
        result = jnp.where(target == want, value, result)
    return result


def placed(rows, cols, read, down, across):
    total = {}
    for c in range(2):
        strips = [[read(c, u, m) for m in range(3)] for u in range(3)]
        for b in across:
            part = [chosen(cols[c], b, strips[u]) for u in range(3)]
            for a in down:
                value = chosen(rows[c], a, part)
                total[a, b] = total[a, b] + value if c else value
    return total


def span(start, size):
    return pl.ds(pl.multiple_of(start * size, size), size)


def lanes(v, j):
    return jnp.take_along_axis(v, jnp.full((8, BS), j, jnp.int32), axis=1)


def sublanes(v, i):
    return jnp.broadcast_to(v[i : i + 1, :], (8, BS))


def factor_block(block, upper, inverse, after):
    row = lax.broadcasted_iota(jnp.int32, (8, BS), 0)
    lane = lax.broadcasted_iota(jnp.int32, (8, BS), 1)
    tiles = BS // LEAF
    wa = [block[8 * t : 8 * t + 8, :] for t in range(tiles)]
    wi = [jnp.where(lane == row + 8 * t, 1.0, 0.0).astype(F32) for t in range(tiles)]
    for t in range(tiles):
        cols = {w: [lanes(wa[w], 8 * t + m) for m in range(8)] for w in range(t, tiles)}
        sc = [[sublanes(cols[t][n], m) if n <= m else None for n in range(8)] for m in range(8)]
        low = [[None] * 8 for _ in range(8)]
        rs, ua, ui = [None] * 8, [None] * 8, [None] * 8
        for m in range(8):
            rs[m] = lax.rsqrt(sc[m][m])
            for i in range(m + 1, 8):
                low[i][m] = sc[i][m] * rs[m]
            for i in range(m + 1, 8):
                for j in range(m + 1, i + 1):
                    sc[i][j] = sc[i][j] - low[i][m] * low[j][m]
            ga, gi = sublanes(wa[t], m), sublanes(wi[t], m)
            for n in range(m):
                ga = ga - low[m][n] * ua[n]
                gi = gi - low[m][n] * ui[n]
            ua[m], ui[m] = ga * rs[m], gi * rs[m]
        up, inv = ua[0], ui[0]
        for m in range(1, 8):
            up = jnp.where(row == m, ua[m], up)
            inv = jnp.where(row == m, ui[m], inv)
        upper[8 * t : 8 * t + 8, :] = jnp.where(lane >= row + 8 * t, up, 0.0)
        inverse[8 * t : 8 * t + 8, :] = jnp.where(lane <= row + 8 * t, inv, 0.0)
        after(t)
        if t == tiles - 1:
            break
        ya, yi = [None] * 8, [None] * 8
        for m in reversed(range(8)):
            a, b = ua[m], ui[m]
            for n in range(m + 1, 8):
                a = a - low[n][m] * ya[n]
                b = b - low[n][m] * yi[n]
            ya[m], yi[m] = a * rs[m], b * rs[m]
        for w in range(t + 1, tiles):
            a, b = wa[w], wi[w]
            for m in range(8):
                a = a - cols[w][m] * ya[m]
                b = b - cols[w][m] * yi[m]
            wa[w], wi[w] = a, b


ROWS_T = ((1,), (1,))
PLAIN = ((1,), (0,))


def kernel(maps, front, children, out, kids, arrived, left, right, corner, work, lows, inverses, uppers, panel, pr,
           col_send, col_mine, row_send, row_mine, first_recv, line_in, plane_in,
           fs, xs, sl, sp, rl, rp, gs, gr, hs, hr, ws, wr, bs, br, ls, cx, cy, cb, cr, cbr, ps, pq):
    s, r, q = position()
    dev_row = 8 * s + r
    x, y, z, core = 2 * lax.rem(r, 2) + s, r // 2, q // 2, lax.rem(q, 2)

    def at_x(d):
        nx = lax.rem(x + 4 + d, 4)
        return (lax.rem(nx, 2), 2 * y + nx // 2, q)

    def at_y(d):
        return (s, 2 * lax.rem(y + 4 + d, 4) + lax.rem(r, 2), q)

    def at_z(d, to_core=core):
        return (s, r, 2 * lax.rem(z + 8 + d, 8) + to_core)

    sibling = (s, r, 2 * z + 1 - core)
    partner = (1 - s, r, q)

    barrier = pltpu.get_barrier_semaphore()
    plane_peers = [(dx, dy) for dx in range(4) for dy in range(4)]
    line_peers = [(dz, c) for dz in range(8) for c in range(2)]

    def in_line(side, dz, c):
        return (side, r, 2 * lax.rem(z + dz, 8) + lax.rem(core + c, 2))

    def in_plane(dx, dy):
        nx = lax.rem(x + dx, 4)
        return (lax.rem(nx, 2), 2 * lax.rem(y + dy, 4) + nx // 2, q)

    peers = [in_line(s, *p) for p in line_peers[1:]] + [in_line(1 - s, *p) for p in line_peers[1:]]
    peers += [in_plane(*p) for p in plane_peers[1:]]
    for peer in peers:
        pl.semaphore_signal(barrier, inc=1, device_id=peer, device_id_type=MESH)
    fetch = [pltpu.make_async_copy(children.at[c], kids.at[c], fs.at[c]) for c in range(2)]
    fetch.append(pltpu.make_async_copy(front, out, fs.at[2]))
    for f in fetch:
        f.start()

    def copy(src, dst, send, recv, device):
        return pltpu.make_async_remote_copy(
            src_ref=src, dst_ref=dst, send_sem=send, recv_sem=recv, device_id=device, device_id_type=MESH
        )

    def rows_of(child, side):
        return [maps[child, (2 * u + side) * 8 + r] // 16 for u in range(3)]

    def cols_of(child):
        return [maps[child, m * 16 + q] // 16 for m in range(3)]

    mine = [(2 * s + c) for c in range(2)]
    cols = [cols_of(child) for child in mine]
    kept = [rows_of(child, s) for child in mine]
    given = [rows_of(child, 1 - s) for child in mine]

    def strips(body):
        @pl.loop(0, BS // 8)
        def _(i):
            body(lambda a: pl.ds(pl.multiple_of(a * BS + 8 * i, 8), 8))

    def own(at, side):
        return lambda c, u, m: kids[c, at(2 * u + side), m * BS : (m + 1) * BS]

    for f in fetch:
        f.wait()

    @pl.when(q < NPB)
    def _():
        @strips
        def _(at):
            sent = placed(given, cols, own(at, 1 - s), range(5), [0])
            stay = placed(kept, cols, own(at, s), range(5), [0])
            for n in range(5):
                col_send[n, at(0), :] = sent[n, 0]
                col_mine[n, at(0), :] = out[at(n), :BS] + stay[n, 0]

    @pl.when(r < NPB)
    def _():
        @strips
        def _(at):
            first = placed([rows_of(child, 0) for child in mine], cols, own(at, 0), [0], range(5))
            for n in range(5):
                row_send[n, at(0), :] = first[0, n]
                row_mine[n, at(0), :] = out[at(0), n * BS : (n + 1) * BS] + first[0, n]

    pl.semaphore_wait(barrier, len(peers))

    def first_copy():
        return copy(col_send.at[0], first_recv, xs.at[0], xs.at[1], partner)

    first_on = (r < NPB) & (q < NPB)

    @pl.when(first_on & (s == 1))
    def _():
        first_copy().start()

    def line_rows(dz, c):
        return pl.ds(pl.multiple_of(HALF * lax.rem(core + c, 2) + 8 * lax.rem(z + dz, 8), 8), 8)

    def plane_rows(dx, dy):
        return pl.ds(pl.multiple_of(32 * lax.rem(y + dy, 4) + 8 * lax.rem(x + dx, 4), 8), 8)

    own_line, own_plane = line_rows(0, 0), plane_rows(0, 0)

    def scatter(act):
        for k in range(NPB):

            @pl.when(q == k)
            def _():
                for j, p in enumerate(line_peers):
                    rows = line_rows(*p)
                    act(copy(col_send.at[:, rows], line_in.at[k, 1], sl.at[1, j], rl.at[k, 1], in_line(1 - s, *p)))
                    if j:
                        act(copy(col_mine.at[:, rows], line_in.at[k, 0], sl.at[0, j], rl.at[k, 0], in_line(s, *p)))

        for i in range(NPB):
            for side, held in ((0, row_mine), (1, row_send)):

                @pl.when((r == i) & (s == side))
                def _():
                    for j, p in enumerate(plane_peers):
                        if j:
                            rows = plane_rows(*p)
                            act(copy(held.at[:, rows], plane_in.at[i, side], sp.at[j], rp.at[i, side], in_plane(*p)))

    def gather_sum():
        for k in range(NPB):
            copy(line_in.at[k, 1], line_in.at[k, 1], sl.at[1, 0], rl.at[k, 1], sibling).wait_recv()

            @pl.when(q == k)
            def _():
                left[k, :, own_line, :] = col_mine[:, own_line, :] + line_in[k, 1]

            @pl.when(q != k)
            def _():
                copy(line_in.at[k, 0], line_in.at[k, 0], sl.at[0, 0], rl.at[k, 0], sibling).wait_recv()
                left[k, :, own_line, :] = line_in[k, 0] + line_in[k, 1]

        for i in range(NPB):
            for side, held in ((0, row_mine), (1, row_send)):
                holder = (r == i) & (s == side)

                @pl.when(holder)
                def _():
                    plane_in[i, side] = held[:, own_plane, :]

                @pl.when(jnp.logical_not(holder))
                def _():
                    copy(plane_in.at[i, side], plane_in.at[i, side], sp.at[0], rp.at[i, side], sibling).wait_recv()

            right[i, :, own_plane, :] = plane_in[i, 0] + plane_in[i, 1]

    def along_z(act):
        here = left.at[:, :, own_line]
        for d in (4, 3, 5, 2, 6, 1, 7):
            act(copy(here, here, gs.at[d], gr.at[d], at_z(d)))

    def along_x(act):
        here = right.at[:, :, own_plane]
        for d in (2, 1, 3):
            act(copy(here, here, hs.at[d], hr.at[d], at_x(d)))

    def along_y(act):
        here = right.at[:, :, span(y, 32)]
        for d in (2, 1, 3):
            act(copy(here, here, ws.at[d], wr.at[d], at_y(d)))

    def to_sibling(act):
        here = left.at[:, :, span(core, HALF)]
        act(copy(here, here, bs.at[0], br.at[0], sibling))

    def pieces(act, children_at=range(2)):
        for c in children_at:
            for u in range(3):
                act(copy(kids.at[c, span(2 * u + 1 - s, BS), :], arrived.at[c, u], ps.at[c, u], pq.at[c, u], partner))

    def add(rows, cols, read):
        @strips
        def _(at):
            total = placed(rows, cols, read(at), range(5), range(5))
            for a in range(5):
                for b in range(5):
                    lanes_b = slice(b * BS, (b + 1) * BS)
                    out[at(a), lanes_b] = out[at(a), lanes_b] + total[a, b]

    add(kept, cols, lambda at: own(at, s))

    corners = [(i, k) for i in range(NPB) for k in range(i + 1)]
    my_half = span(core, HALF)
    far_z = (4, 3, 5, 2, 6, 1, 7)

    def corner_stage(i):
        _, yi = SOURCE[i]
        at_line = dev_row == i
        return at_line, y == yi

    def corner_line(i, k, act):
        for d in range(7):
            for c in range(2):
                part = corner.at[i, k, c * HALF : (c + 1) * HALF, :]
                act(copy(part, part, ls.at[2 * d + c], cr.at[i, k], at_z(far_z[d], c)))
        part = corner.at[i, k, span(1 - core, HALF), :]
        act(copy(part, part, ls.at[14], cr.at[i, k], sibling))

    def corner_sends(i, k, act):
        at_line, at_row = corner_stage(i)
        part = corner.at[i, k, my_half, :]

        @pl.when(at_line & (q == k))
        def _():
            corner_line(i, k, act)

        @pl.when(at_line)
        def _():
            for d in (2, 1, 3):
                act(copy(part, part, cx.at[i, k, d], cr.at[i, k], at_x(d)))

        @pl.when(at_row)
        def _():
            for d in (2, 1, 3):
                act(copy(part, part, cy.at[i, k, d], cr.at[i, k], at_y(d)))

        @pl.when(jnp.logical_not(at_line & (q == k ^ 1)))
        def _():
            act(copy(part, part, cb.at[i, k], cbr.at[i, k], sibling))

    def corner_step(i, k, stage):
        at_line, at_row = corner_stage(i)
        mine_now = (at_line & (q == k), at_line & (q != k), at_row & jnp.logical_not(at_line), jnp.logical_not(at_row))

        @pl.when(mine_now[stage])
        def _():
            if stage == 0:
                first_copy().wait_recv()
                corner[i, k] = col_mine[0] + first_recv[...]
            else:
                part = corner.at[i, k, my_half, :]
                copy(part, part, cb.at[i, k], cr.at[i, k], sibling).wait_recv()
            corner_sends(i, k, lambda c: c.start())

    @pl.when(first_on & (s == 0) & (q > r))
    def _():
        first_copy().wait_recv()

    for stage in range(4):
        for i, k in corners:
            corner_step(i, k, stage)
        if stage == 0:
            scatter(lambda c: c.start())

        if stage < 2:

            @pl.when(((s == 0) & (r < NPB)) == (stage == 1))
            def _():
                pieces(lambda c: c.start(), [0])

        if stage == SUM_AFTER:
            gather_sum()
            along_x(lambda c: c.start())
            along_z(lambda c: c.start())
            pieces(lambda c: c.start(), [1])
    for i, k in corners:
        other = corner.at[i, k, span(1 - core, HALF), :]

        @pl.when(jnp.logical_not((dev_row == i) & (q == k)))
        def _():
            copy(other, other, cb.at[i, k], cbr.at[i, k], sibling).wait_recv()

        work[i, k] = corner[i, k]

    @pl.loop(0, NPB)
    def _(k):
        def after(t):
            if t == Y_AT[1]:

                @pl.when(k == Y_AT[0])
                def _():
                    along_x(lambda c: c.wait_recv())
                    along_y(lambda c: c.start())

            if t == Z_AT[1]:

                @pl.when(k == Z_AT[0])
                def _():
                    along_z(lambda c: c.wait_recv())
                    to_sibling(lambda c: c.start())

        factor_block(work.at[k, k], uppers.at[k], inverses.at[k], after)
        inv = inverses[k]
        for i in range(1, NPB):

            @pl.when(i > k)
            def _():
                lows[i, k] = dot(work[i, k], inv, ROWS_T)

        for i in range(1, NPB):
            for j in range(1, i + 1):

                @pl.when(j > k)
                def _():
                    work[i, j] = work[i, j] - dot(lows[i, k], lows[j, k], ROWS_T)

    along_y(lambda c: c.wait_recv())
    to_sibling(lambda c: c.wait_recv())

    columns, rows = [], [[] for _ in range(5)]
    low = {(k, i): split(lows[k, i]) for k in range(NPB) for i in range(k)}
    for k in range(NPB):
        inv = split(inverses[k])
        own = left[k].reshape(5 * BS, BS)
        for i in range(k):
            own = own - dot3(columns[i], low[k, i], ROWS_T)
        own = dot3(split(own), inv, ROWS_T)
        panel[:, k * BS : (k + 1) * BS] = own
        columns.append(split(own))
        for n in range(5):
            other = right[k, n]
            for i in range(k):
                other = other - dot3(low[k, i], rows[n][i], PLAIN)
            other = dot3(inv, split(other), PLAIN)
            pr[k * BS : (k + 1) * BS, n * BS : (n + 1) * BS] = other
            rows[n].append(split(other))

    across = split(pr[...])
    for a in range(5):
        strip = slice(a * BS, (a + 1) * BS)
        out[strip, :] = out[strip, :] - dot3(split(panel[strip, :]), across, PLAIN)

    pieces(lambda c: c.wait())

    theirs = [2 * (1 - s) + c for c in range(2)]
    add(
        [rows_of(child, s) for child in theirs],
        [cols_of(child) for child in theirs],
        lambda at: lambda c, u, m: arrived[c, u, at(0), m * BS : (m + 1) * BS],
    )

    for k in range(NPB):

        @pl.when(q == k)
        def _():
            out[BS:, :BS] = panel[BS:, k * BS : (k + 1) * BS]

            @pl.when(dev_row > k)
            def _():
                out[:BS, :BS] = panel[:BS, k * BS : (k + 1) * BS]

            @pl.when(dev_row == k)
            def _():
                out[:BS, :BS] = uppers[k].T

    @pl.when(first_on & (s == 1))
    def _():
        first_copy().wait_send()

    scatter(lambda c: c.wait_send())
    for act in (along_x, along_y, along_z, to_sibling):
        act(lambda c: c.wait_send())
    for i, k in corners:
        corner_sends(i, k, lambda c: c.wait_send())


def body(front, children, child_maps):
    dma = pltpu.SemaphoreType.DMA

    def vmem(*dims):
        return pltpu.VMEM(dims, F32)

    done = pl.pallas_call(
        kernel,
        out_shape=jax.ShapeDtypeStruct((5 * BS, 5 * BS), F32),
        in_specs=[SMEM, ANY, ANY],
        out_specs=VMEM,
        scratch_shapes=[
            vmem(2, 6 * BS, 3 * BS),
            vmem(2, 3, BS, 3 * BS),
            vmem(NPB, 5, BS, BS),
            vmem(NPB, 5, BS, BS),
            vmem(NPB, NPB, BS, BS),
            vmem(NPB, NPB, BS, BS),
            vmem(NPB, NPB, BS, BS),
            vmem(NPB, BS, BS),
            vmem(NPB, BS, BS),
            vmem(5 * BS, NPB * BS),
            vmem(NPB * BS, 5 * BS),
        ]
        + [vmem(5, BS, BS)] * 4
        + [vmem(BS, BS), vmem(NPB, 2, 5, 8, BS), vmem(NPB, 2, 5, 8, BS)]
        + [
            dma((3,)),
            dma((2,)),
            dma((2, 16)),
            dma((16,)),
            dma((NPB, 2)),
            dma((NPB, 2)),
            dma((8,)),
            dma((8,)),
            dma((4,)),
            dma((4,)),
            dma((4,)),
            dma((4,)),
            dma((1,)),
            dma((1,)),
            dma((15,)),
            dma((NPB, NPB, 4)),
            dma((NPB, NPB, 4)),
            dma((NPB, NPB)),
            dma((NPB, NPB)),
            dma((NPB, NPB)),
            dma((2, 3)),
            dma((2, 3)),
        ],
        compiler_params=pltpu.CompilerParams(collective_id=0, has_side_effects=True),
        name="front",
    )(child_maps, front, children)
    s, r, q = position()
    section = 8 * s + r
    row = lax.broadcasted_iota(jnp.int32, done.shape, 0)
    column = lax.broadcasted_iota(jnp.int32, done.shape, 1)
    return jnp.where((section < NPB) & (row < BS) & (column // BS * 16 + q > section), 0.0, done)


def solution(mesh):
    return jax.shard_map(
        body,
        mesh=mesh,
        in_specs=(P(("sub", "row"), "col"), P("sub", "row", "col"), P()),
        out_specs=P(("sub", "row"), "col"),
        check_vma=False,
    )
```

```python
import jax
import jax.numpy as jnp
from jax import lax
from jax.experimental import pallas as pl
from jax.experimental.pallas import tpu as pltpu
from jax.sharding import PartitionSpec as P

BS = 128
NPB = 3
LEAF = 8
SUM_AFTER = 1
Z_AT = (1, 4)
F32 = jnp.float32
MESH = pl.DeviceIdType.MESH
HIGHEST = lax.Precision.HIGHEST
VMEM = pl.BlockSpec(memory_space=pltpu.VMEM)
SMEM = pl.BlockSpec(memory_space=pltpu.SMEM)
ANY = pl.BlockSpec(memory_space=pl.ANY)
SOURCE = ((0, 0), (2, 0), (0, 1))
HALF = BS // 2


def position():
    return lax.axis_index("sub"), lax.axis_index("row"), lax.axis_index("col")


def split(a):
    high = a.astype(jnp.bfloat16)
    return high, (a - high.astype(F32)).astype(jnp.bfloat16)


def dot3(a, b, dims):
    def part(u, v):
        return lax.dot_general(u, v, (dims, ((), ())), preferred_element_type=F32)

    return part(a[0], b[0]) + (part(a[0], b[1]) + part(a[1], b[0]))


def dot(a, b, dims):
    return lax.dot_general(a, b, (dims, ((), ())), precision=HIGHEST, preferred_element_type=F32)


def chosen(targets, want, values):
    result = jnp.zeros_like(values[0])
    for target, value in zip(targets, values):
        result = jnp.where(target == want, value, result)
    return result


def placed(rows, cols, read, down, across):
    total = {}
    for c in range(2):
        strips = [[read(c, u, m) for m in range(3)] for u in range(3)]
        for b in across:
            part = [chosen(cols[c], b, strips[u]) for u in range(3)]
            for a in down:
                value = chosen(rows[c], a, part)
                total[a, b] = total[a, b] + value if c else value
    return total


def span(start, size):
    return pl.ds(pl.multiple_of(start * size, size), size)


def lanes(v, j):
    return jnp.take_along_axis(v, jnp.full((8, BS), j, jnp.int32), axis=1)


def sublanes(v, i):
    return jnp.broadcast_to(v[i : i + 1, :], (8, BS))


def factor_block(block, upper, inverse, after):
    row = lax.broadcasted_iota(jnp.int32, (8, BS), 0)
    lane = lax.broadcasted_iota(jnp.int32, (8, BS), 1)
    tiles = BS // LEAF
    wa = [block[8 * t : 8 * t + 8, :] for t in range(tiles)]
    wi = [jnp.where(lane == row + 8 * t, 1.0, 0.0).astype(F32) for t in range(tiles)]
    for t in range(tiles):
        cols = {w: [lanes(wa[w], 8 * t + m) for m in range(8)] for w in range(t, tiles)}
        sc = [[sublanes(cols[t][n], m) if n <= m else None for n in range(8)] for m in range(8)]
        low = [[None] * 8 for _ in range(8)]
        rs, ua, ui = [None] * 8, [None] * 8, [None] * 8
        for m in range(8):
            rs[m] = lax.rsqrt(sc[m][m])
            for i in range(m + 1, 8):
                low[i][m] = sc[i][m] * rs[m]
            for i in range(m + 1, 8):
                for j in range(m + 1, i + 1):
                    sc[i][j] = sc[i][j] - low[i][m] * low[j][m]
            ga, gi = sublanes(wa[t], m), sublanes(wi[t], m)
            for n in range(m):
                ga = ga - low[m][n] * ua[n]
                gi = gi - low[m][n] * ui[n]
            ua[m], ui[m] = ga * rs[m], gi * rs[m]
        up, inv = ua[0], ui[0]
        for m in range(1, 8):
            up = jnp.where(row == m, ua[m], up)
            inv = jnp.where(row == m, ui[m], inv)
        upper[8 * t : 8 * t + 8, :] = jnp.where(lane >= row + 8 * t, up, 0.0)
        inverse[8 * t : 8 * t + 8, :] = jnp.where(lane <= row + 8 * t, inv, 0.0)
        after(t)
        if t == tiles - 1:
            break
        ya, yi = [None] * 8, [None] * 8
        for m in reversed(range(8)):
            a, b = ua[m], ui[m]
            for n in range(m + 1, 8):
                a = a - low[n][m] * ya[n]
                b = b - low[n][m] * yi[n]
            ya[m], yi[m] = a * rs[m], b * rs[m]
        for w in range(t + 1, tiles):
            a, b = wa[w], wi[w]
            for m in range(8):
                a = a - cols[w][m] * ya[m]
                b = b - cols[w][m] * yi[m]
            wa[w], wi[w] = a, b


ROWS_T = ((1,), (1,))
PLAIN = ((1,), (0,))


def kernel(maps, front, children, out, kids, arrived, left, right, corner, work, lows, inverses, uppers, panel, pr,
           col_send, col_mine, row_send, row_mine, first_recv, line_in, plane_in,
           fs, xs, sl, sp, rl, rp, gs, gr, hs, hr, ws, wr, bs, br, ls, cx, cy, cb, cr, cbr, ps, pq):
    s, r, q = position()
    dev_row = 8 * s + r
    x, y, z, core = 2 * lax.rem(r, 2) + s, r // 2, q // 2, lax.rem(q, 2)

    def at_x(d):
        nx = lax.rem(x + 4 + d, 4)
        return (lax.rem(nx, 2), 2 * y + nx // 2, q)

    def at_y(d):
        return (s, 2 * lax.rem(y + 4 + d, 4) + lax.rem(r, 2), q)

    def at_z(d, to_core=core):
        return (s, r, 2 * lax.rem(z + 8 + d, 8) + to_core)

    sibling = (s, r, 2 * z + 1 - core)
    partner = (1 - s, r, q)

    barrier = pltpu.get_barrier_semaphore()
    plane_peers = [(dx, dy) for dx in range(4) for dy in range(4)]
    line_peers = [(dz, c) for dz in range(8) for c in range(2)]

    def in_line(side, dz, c):
        return (side, r, 2 * lax.rem(z + dz, 8) + lax.rem(core + c, 2))

    def in_plane(dx, dy):
        nx = lax.rem(x + dx, 4)
        return (lax.rem(nx, 2), 2 * lax.rem(y + dy, 4) + nx // 2, q)

    peers = [in_line(s, *p) for p in line_peers[1:]] + [in_line(1 - s, *p) for p in line_peers[1:]]
    peers += [in_plane(*p) for p in plane_peers[1:]]
    for peer in peers:
        pl.semaphore_signal(barrier, inc=1, device_id=peer, device_id_type=MESH)
    fetch = [pltpu.make_async_copy(children.at[c], kids.at[c], fs.at[c]) for c in range(2)]
    fetch.append(pltpu.make_async_copy(front, out, fs.at[2]))
    for f in fetch:
        f.start()

    def copy(src, dst, send, recv, device):
        return pltpu.make_async_remote_copy(
            src_ref=src, dst_ref=dst, send_sem=send, recv_sem=recv, device_id=device, device_id_type=MESH
        )

    def rows_of(child, side):
        return [maps[child, (2 * u + side) * 8 + r] // 16 for u in range(3)]

    def cols_of(child):
        return [maps[child, m * 16 + q] // 16 for m in range(3)]

    mine = [(2 * s + c) for c in range(2)]
    cols = [cols_of(child) for child in mine]
    kept = [rows_of(child, s) for child in mine]
    given = [rows_of(child, 1 - s) for child in mine]

    def strips(body):
        @pl.loop(0, BS // 8)
        def _(i):
            body(lambda a: pl.ds(pl.multiple_of(a * BS + 8 * i, 8), 8))

    def own(at, side):
        return lambda c, u, m: kids[c, at(2 * u + side), m * BS : (m + 1) * BS]

    for f in fetch:
        f.wait()

    @pl.when(q < NPB)
    def _():
        @strips
        def _(at):
            sent = placed(given, cols, own(at, 1 - s), range(5), [0])
            stay = placed(kept, cols, own(at, s), range(5), [0])
            for n in range(5):
                col_send[n, at(0), :] = sent[n, 0]
                col_mine[n, at(0), :] = out[at(n), :BS] + stay[n, 0]

    @pl.when(r < NPB)
    def _():
        @strips
        def _(at):
            first = placed([rows_of(child, 0) for child in mine], cols, own(at, 0), [0], range(5))
            for n in range(5):
                row_send[n, at(0), :] = first[0, n]
                row_mine[n, at(0), :] = out[at(0), n * BS : (n + 1) * BS] + first[0, n]

    pl.semaphore_wait(barrier, len(peers))

    def first_copy():
        return copy(col_send.at[0], first_recv, xs.at[0], xs.at[1], partner)

    first_on = (r < NPB) & (q < NPB)

    @pl.when(first_on & (s == 1))
    def _():
        first_copy().start()

    def line_rows(dz, c):
        return pl.ds(pl.multiple_of(HALF * lax.rem(core + c, 2) + 8 * lax.rem(z + dz, 8), 8), 8)

    def plane_rows(dx, dy):
        return pl.ds(pl.multiple_of(32 * lax.rem(y + dy, 4) + 8 * lax.rem(x + dx, 4), 8), 8)

    own_line, own_plane = line_rows(0, 0), plane_rows(0, 0)

    def scatter(act):
        for k in range(NPB):

            @pl.when(q == k)
            def _():
                for j, p in enumerate(line_peers):
                    rows = line_rows(*p)
                    act(copy(col_send.at[:, rows], line_in.at[k, 1], sl.at[1, j], rl.at[k, 1], in_line(1 - s, *p)))
                    if j:
                        act(copy(col_mine.at[:, rows], line_in.at[k, 0], sl.at[0, j], rl.at[k, 0], in_line(s, *p)))

        for i in range(NPB):
            for side, held in ((0, row_mine), (1, row_send)):

                @pl.when((r == i) & (s == side))
                def _():
                    for j, p in enumerate(plane_peers):
                        if j:
                            rows = plane_rows(*p)
                            act(copy(held.at[:, rows], plane_in.at[i, side], sp.at[j], rp.at[i, side], in_plane(*p)))

    def gather_sum():
        for k in range(NPB):
            copy(line_in.at[k, 1], line_in.at[k, 1], sl.at[1, 0], rl.at[k, 1], sibling).wait_recv()

            @pl.when(q == k)
            def _():
                left[k, :, own_line, :] = col_mine[:, own_line, :] + line_in[k, 1]

            @pl.when(q != k)
            def _():
                copy(line_in.at[k, 0], line_in.at[k, 0], sl.at[0, 0], rl.at[k, 0], sibling).wait_recv()
                left[k, :, own_line, :] = line_in[k, 0] + line_in[k, 1]

        for i in range(NPB):
            for side, held in ((0, row_mine), (1, row_send)):
                holder = (r == i) & (s == side)

                @pl.when(holder)
                def _():
                    plane_in[i, side] = held[:, own_plane, :]

                @pl.when(jnp.logical_not(holder))
                def _():
                    copy(plane_in.at[i, side], plane_in.at[i, side], sp.at[0], rp.at[i, side], sibling).wait_recv()

            right[i, :, own_plane, :] = plane_in[i, 0] + plane_in[i, 1]

    def along_z(act):
        here = left.at[:, :, own_line]
        for d in (4, 3, 5, 2, 6, 1, 7):
            act(copy(here, here, gs.at[d], gr.at[d], at_z(d)))

    def along_x(act):
        here = right.at[:, :, own_plane]
        for d in (2, 1, 3):
            act(copy(here, here, hs.at[d], hr.at[d], at_x(d)))

    def along_y(act):
        here = right.at[:, :, span(y, 32)]
        for d in (2, 1, 3):
            act(copy(here, here, ws.at[d], wr.at[d], at_y(d)))

    def to_sibling(act):
        here = left.at[:, :, span(core, HALF)]
        act(copy(here, here, bs.at[0], br.at[0], sibling))

    def pieces(act, children_at=range(2)):
        for c in children_at:
            for u in range(3):
                act(copy(kids.at[c, span(2 * u + 1 - s, BS), :], arrived.at[c, u], ps.at[c, u], pq.at[c, u], partner))

    def add(rows, cols, read):
        @strips
        def _(at):
            total = placed(rows, cols, read(at), range(5), range(5))
            for a in range(5):
                for b in range(5):
                    lanes_b = slice(b * BS, (b + 1) * BS)
                    out[at(a), lanes_b] = out[at(a), lanes_b] + total[a, b]

    add(kept, cols, lambda at: own(at, s))

    corners = [(i, k) for i in range(NPB) for k in range(i + 1)]
    my_half = span(core, HALF)
    far_z = (4, 3, 5, 2, 6, 1, 7)

    def corner_stage(i):
        _, yi = SOURCE[i]
        at_line = dev_row == i
        return at_line, y == yi

    def corner_line(i, k, act):
        for d in range(7):
            for c in range(2):
                part = corner.at[i, k, c * HALF : (c + 1) * HALF, :]
                act(copy(part, part, ls.at[2 * d + c], cr.at[i, k], at_z(far_z[d], c)))
        part = corner.at[i, k, span(1 - core, HALF), :]
        act(copy(part, part, ls.at[14], cr.at[i, k], sibling))

    def corner_sends(i, k, act):
        at_line, at_row = corner_stage(i)
        part = corner.at[i, k, my_half, :]

        @pl.when(at_line & (q == k))
        def _():
            corner_line(i, k, act)

        @pl.when(at_line)
        def _():
            for d in (2, 1, 3):
                act(copy(part, part, cx.at[i, k, d], cr.at[i, k], at_x(d)))

        @pl.when(at_row)
        def _():
            for d in (2, 1, 3):
                act(copy(part, part, cy.at[i, k, d], cr.at[i, k], at_y(d)))

        @pl.when(jnp.logical_not(at_line & (q == k ^ 1)))
        def _():
            act(copy(part, part, cb.at[i, k], cbr.at[i, k], sibling))

    def corner_step(i, k, stage):
        at_line, at_row = corner_stage(i)
        mine_now = (at_line & (q == k), at_line & (q != k), at_row & jnp.logical_not(at_line), jnp.logical_not(at_row))

        @pl.when(mine_now[stage])
        def _():
            if stage == 0:
                first_copy().wait_recv()
                corner[i, k] = col_mine[0] + first_recv[...]
            else:
                part = corner.at[i, k, my_half, :]
                copy(part, part, cb.at[i, k], cr.at[i, k], sibling).wait_recv()
            corner_sends(i, k, lambda c: c.start())

    @pl.when(first_on & (s == 0) & (q > r))
    def _():
        first_copy().wait_recv()

    for stage in range(4):
        for i, k in corners:
            corner_step(i, k, stage)
        if stage == 0:
            scatter(lambda c: c.start())

        if stage < 2:

            @pl.when(((s == 0) & (r < NPB)) == (stage == 1))
            def _():
                pieces(lambda c: c.start(), [0])

        if stage == SUM_AFTER:
            gather_sum()
            along_x(lambda c: c.start())
            along_z(lambda c: c.start())
            pieces(lambda c: c.start(), [1])
    along_x(lambda c: c.wait_recv())
    along_y(lambda c: c.start())
    for i, k in corners:
        other = corner.at[i, k, span(1 - core, HALF), :]

        @pl.when(jnp.logical_not((dev_row == i) & (q == k)))
        def _():
            copy(other, other, cb.at[i, k], cbr.at[i, k], sibling).wait_recv()

        work[i, k] = corner[i, k]

    @pl.loop(0, NPB)
    def _(k):
        def after(t):
            if t == Z_AT[1]:

                @pl.when(k == Z_AT[0])
                def _():
                    along_z(lambda c: c.wait_recv())
                    to_sibling(lambda c: c.start())

        factor_block(work.at[k, k], uppers.at[k], inverses.at[k], after)
        inv = inverses[k]
        for i in range(1, NPB):

            @pl.when(i > k)
            def _():
                lows[i, k] = dot(work[i, k], inv, ROWS_T)

        for i in range(1, NPB):
            for j in range(1, i + 1):

                @pl.when(j > k)
                def _():
                    work[i, j] = work[i, j] - dot(lows[i, k], lows[j, k], ROWS_T)

    along_y(lambda c: c.wait_recv())
    to_sibling(lambda c: c.wait_recv())

    columns, rows = [], [[] for _ in range(5)]
    low = {(k, i): split(lows[k, i]) for k in range(NPB) for i in range(k)}
    for k in range(NPB):
        inv = split(inverses[k])
        own = left[k].reshape(5 * BS, BS)
        for i in range(k):
            own = own - dot3(columns[i], low[k, i], ROWS_T)
        own = dot3(split(own), inv, ROWS_T)
        panel[:, k * BS : (k + 1) * BS] = own
        columns.append(split(own))
        for n in range(5):
            other = right[k, n]
            for i in range(k):
                other = other - dot3(low[k, i], rows[n][i], PLAIN)
            other = dot3(inv, split(other), PLAIN)
            pr[k * BS : (k + 1) * BS, n * BS : (n + 1) * BS] = other
            rows[n].append(split(other))

    across = split(pr[...])
    for a in range(5):
        strip = slice(a * BS, (a + 1) * BS)
        out[strip, :] = out[strip, :] - dot3(split(panel[strip, :]), across, PLAIN)

    pieces(lambda c: c.wait())

    theirs = [2 * (1 - s) + c for c in range(2)]
    add(
        [rows_of(child, s) for child in theirs],
        [cols_of(child) for child in theirs],
        lambda at: lambda c, u, m: arrived[c, u, at(0), m * BS : (m + 1) * BS],
    )

    for k in range(NPB):

        @pl.when(q == k)
        def _():
            out[BS:, :BS] = panel[BS:, k * BS : (k + 1) * BS]

            @pl.when(dev_row > k)
            def _():
                out[:BS, :BS] = panel[:BS, k * BS : (k + 1) * BS]

            @pl.when(dev_row == k)
            def _():
                out[:BS, :BS] = uppers[k].T

    @pl.when(first_on & (s == 1))
    def _():
        first_copy().wait_send()

    scatter(lambda c: c.wait_send())
    for act in (along_x, along_y, along_z, to_sibling):
        act(lambda c: c.wait_send())
    for i, k in corners:
        corner_sends(i, k, lambda c: c.wait_send())


def clear_kernel(done, out):
    s, r, q = position()
    section = 8 * s + r
    column = lax.broadcasted_iota(jnp.int32, done.shape, 1) // BS * 16 + q
    pivot = (pl.program_id(0) == 0) & (section < NPB)
    out[...] = jnp.where(pivot & (column > section), 0.0, done[...])


def body(front, children, child_maps):
    dma = pltpu.SemaphoreType.DMA

    def vmem(*dims):
        return pltpu.VMEM(dims, F32)

    done = pl.pallas_call(
        kernel,
        out_shape=jax.ShapeDtypeStruct((5 * BS, 5 * BS), F32),
        in_specs=[SMEM, ANY, ANY],
        out_specs=VMEM,
        scratch_shapes=[
            vmem(2, 6 * BS, 3 * BS),
            vmem(2, 3, BS, 3 * BS),
            vmem(NPB, 5, BS, BS),
            vmem(NPB, 5, BS, BS),
            vmem(NPB, NPB, BS, BS),
            vmem(NPB, NPB, BS, BS),
            vmem(NPB, NPB, BS, BS),
            vmem(NPB, BS, BS),
            vmem(NPB, BS, BS),
            vmem(5 * BS, NPB * BS),
            vmem(NPB * BS, 5 * BS),
        ]
        + [vmem(5, BS, BS)] * 4
        + [vmem(BS, BS), vmem(NPB, 2, 5, 8, BS), vmem(NPB, 2, 5, 8, BS)]
        + [
            dma((3,)),
            dma((2,)),
            dma((2, 16)),
            dma((16,)),
            dma((NPB, 2)),
            dma((NPB, 2)),
            dma((8,)),
            dma((8,)),
            dma((4,)),
            dma((4,)),
            dma((4,)),
            dma((4,)),
            dma((1,)),
            dma((1,)),
            dma((15,)),
            dma((NPB, NPB, 4)),
            dma((NPB, NPB, 4)),
            dma((NPB, NPB)),
            dma((NPB, NPB)),
            dma((NPB, NPB)),
            dma((2, 3)),
            dma((2, 3)),
        ],
        compiler_params=pltpu.CompilerParams(collective_id=0, has_side_effects=True),
        name="front",
    )(child_maps, front, children)
    strip = pl.BlockSpec((BS, 5 * BS), lambda i: (i, 0))
    return pl.pallas_call(
        clear_kernel,
        grid=(5,),
        out_shape=jax.ShapeDtypeStruct(done.shape, F32),
        in_specs=[strip],
        out_specs=strip,
        name="clear",
    )(done)


def solution(mesh):
    return jax.shard_map(
        body,
        mesh=mesh,
        in_specs=(P(("sub", "row"), "col"), P("sub", "row", "col"), P()),
        out_specs=P(("sub", "row"), "col"),
        check_vma=False,
    )
```
